32 devices in a mesh: groups: 2 (over y), ctx: 4 (over z), head: 4 (over x, core).
Axes of the slice: x: 2, y: 2, z: 4, core: 2. Of those that a mesh axis runs over, the one named last changes fastest.
Arguments:
- queries: bfloat16 [4096, 4096], P(('groups', 'ctx', 'head')), parts along dimension 0, may hold values from -6 to 6
- keys_in: bfloat16 [4096, 4096], P(('groups', 'ctx', 'head')), parts along dimension 0, may hold values from -6 to 6
- values: bfloat16 [4096, 4096], P(('groups', 'ctx', 'head')), parts along dimension 0, may hold values from -6 to 6
- doc_lengths: int32 [10], P('groups'), parts along dimension 0, may hold values from 1 to 512, 2048 in all
- rms_gain: float32 [4096], replicated, may hold values from 0.1 to 1.9
Outputs:
- mixed: bfloat16 [4096, 4096], P(('groups', 'ctx', 'head')), parts along dimension 0
The draws below stay inside these ranges and needn't reach their ends.
There are 2 independent parts, one for each index of `groups`. The reference program is written for one: setup_inputs(seed, part) draws one part's arguments, and reference() takes and returns one part's arrays. A program takes and returns all parts, laid end to end along the dimension named above; an argument that names none is the same for every part. Nothing has to cross between parts.
Inputs may be any that keep to these rules, and one draw needn't show every extreme that they name: `doc_lengths`: the lengths of the 5 documents sum to 2048, and the longest has exactly 512 tokens.
All inputs are finite; a program needn't handle non-finite values.
Results may differ from the reference program's by a relative error of at most 0.006.
Values may be sent and summed in bfloat16 or wider, within the bound.
A program may use at most 64 MiB of HBM per device.

```python
import math
import jax
import jax.numpy as jnp
import numpy as np
from jax import lax

H = 32
DH = 128
SHARD = 512
TOKENS = 2048
MOST_DOC = 512
DOCS = 5
N_CTX = 4


def level_of(own_key, extent, cuts, low, largest):
    factor_of, own = 1.0, jax.random.fold_in(own_key, 6)
    for position, shards_of in cuts:
        heights = jnp.exp(jax.random.uniform(jax.random.fold_in(own, position), (shards_of,), jnp.float32, low / len(cuts), largest / len(cuts)))
        factor_of = factor_of * jnp.repeat(heights, extent[position] // shards_of).reshape([-1 if axis == position else 1 for axis in range(len(extent))])
    return factor_of


def length_profile(amount, total, most, skew):
    weights = [(1 << 20) // math.isqrt(rank ** skew) + 1 for rank in range(2, amount + 1)]
    spare, counts = total - most - (amount - 1), [1] * (amount - 1)
    while spare > 0:
        candidates = [i for i in range(amount - 1) if counts[i] < most]
        mass, left = sum([weights[i] for i in candidates]), spare
        for i in candidates:
            extra = min(most - counts[i], max(1, left * weights[i] // mass), spare)
            counts[i] = counts[i] + extra
            spare = spare - extra
    return np.array([most] + counts)


def ragged(key, number_of, total, reach, skew):
    if number_of == 2:
        one = jax.random.randint(key, (), max(1, total - reach), min(reach, total - 1) + 1)
        return jnp.stack([one, total - one])
    lengths = jnp.asarray(length_profile(number_of, total, reach, skew), jnp.int32)
    twos = (number_of - 1) // 2
    donor, taker = lengths[1:1 + 2 * twos:2], lengths[2:2 + 2 * twos:2]
    room = jnp.minimum(donor - 1, reach - taker)
    passed = jax.random.randint(jax.random.fold_in(key, 1), (twos,), 0, 1 << 20) % (room + 1)
    lengths = lengths.at[1:1 + 2 * twos:2].set(donor - passed).at[2:2 + 2 * twos:2].set(taker + passed)
    return lengths[jax.random.permutation(jax.random.fold_in(key, 2), number_of)]


def bell_draw(key, shape, spread, bound, split=(), kind=jnp.bfloat16):
    result = spread * jax.random.normal(key, shape, jnp.float32)
    if split:
        result = result * level_of(key, shape, split, -0.22, 0.18)
    return jnp.clip(result, -bound, bound).astype(kind)


def setup_inputs(seed: int = 0, part: int = 0) -> dict:
    keys = jax.random.split(jax.random.key(seed), 6)
    part_keys = jax.random.split(jax.random.fold_in(keys[5], part), 6)
    return {
        "queries": bell_draw(part_keys[0], (TOKENS, H * DH), 1.0, 6.0, ((0, 16),)),
        "keys_in": bell_draw(part_keys[1], (TOKENS, H * DH), 1.0, 6.0, ((0, 16),)),
        "values": bell_draw(part_keys[2], (TOKENS, H * DH), 1.0, 6.0, ((0, 16),)),
        "doc_lengths": ragged(part_keys[3], DOCS, TOKENS, MOST_DOC, 1).astype(jnp.int32),
        "rms_gain": jnp.clip(1.0 + 0.18 * jax.random.normal(keys[4], (H * DH,), jnp.float32), 0.1, 1.9),
    }


def doc_ids(doc_lengths, positions):
    doc_ends = jnp.cumsum(doc_lengths).astype(jnp.int32)
    counted = lax.optimization_barrier(jnp.sum((positions[:, None] >= doc_ends[None, :]).astype(jnp.int32), axis=1))
    return jnp.where(positions < 0, -1, counted).astype(jnp.int32)

def local_part(q_shard, k_shard, v_shard, segment):
    shard_rows = q_shard.shape[0]
    block_rows = min(512, shard_rows)
    order = jnp.arange(shard_rows, dtype=jnp.int32)
    pieces = []
    for block_id in range(shard_rows // block_rows):
        first_row = block_id * block_rows
        last_row = first_row + block_rows
        scores = jnp.einsum('qhd,khd->hqk', q_shard[first_row:last_row].astype(jnp.float32), k_shard[:last_row].astype(jnp.float32), precision=lax.Precision.HIGHEST)
        allowed = (segment[first_row:last_row, None] == segment[None, :last_row]) & (order[first_row:last_row, None] >= order[None, :last_row])
        weights = jnp.where(allowed[None], scores, 0.0).astype(jnp.bfloat16)
        weights = lax.optimization_barrier(weights)
        pieces.append(jnp.einsum('hqk,khd->qhd', weights.astype(jnp.float32), v_shard[:last_row].astype(jnp.float32), precision=lax.Precision.HIGHEST))
    return jnp.concatenate(pieces, axis=0)

def reference(queries, keys_in, values, doc_lengths, rms_gain):
    shape_four = (N_CTX, SHARD, H, DH)
    q_all = jax.nn.silu(queries.astype(jnp.float32)).astype(jnp.bfloat16).reshape(shape_four)
    k_all = jax.nn.silu(keys_in.astype(jnp.float32)).astype(jnp.bfloat16).reshape(shape_four)
    v_all = values.reshape(shape_four)

    def shard_step(carried, inputs):
        q_shard, k_shard, v_shard, shard_id = inputs
        shard_start = (shard_id * SHARD).astype(jnp.int32)
        positions = shard_start + jnp.arange(SHARD, dtype=jnp.int32)
        segment = doc_ids(doc_lengths, positions)
        before = doc_ids(doc_lengths, jnp.reshape(shard_start - 1, (1,)).astype(jnp.int32))[0]
        local = local_part(q_shard, k_shard, v_shard, segment)
        inter = jnp.einsum('shd,hde->she', q_shard.astype(jnp.float32), carried, precision=lax.Precision.HIGHEST)
        joined = (segment == before)[:, None, None]
        attended = (local + jnp.where(joined, inter, 0.0)).astype(jnp.bfloat16)
        keep = (segment == segment[-1])[:, None, None]
        masked_keys = jnp.where(keep, k_shard, jnp.zeros_like(k_shard))
        tail = jnp.einsum('shd,she->hde', masked_keys.astype(jnp.float32), v_shard.astype(jnp.float32), precision=lax.Precision.HIGHEST)
        carried = jnp.where(segment[-1] != before, tail, carried + tail)
        return (carried, attended)
    start_state = jnp.zeros((H, DH, DH), jnp.float32)
    final_state, attended = lax.scan(shard_step, start_state, (q_all, k_all, v_all, jnp.arange(N_CTX, dtype=jnp.int32)))
    output = attended.reshape(TOKENS, H * DH).astype(jnp.float32)
    meansq = lax.optimization_barrier(jnp.mean(output * output, axis=1, keepdims=True))
    return (output * lax.rsqrt(meansq + 1e-05) * rms_gain.astype(jnp.float32)).astype(jnp.bfloat16)
```

```python
import functools

import jax
import jax.numpy as jnp
from jax import lax
from jax.experimental import pallas as pl
from jax.experimental.pallas import tpu as pltpu
from jax.sharding import PartitionSpec as P

DH = 128
MESH = pl.DeviceIdType.MESH
LIMIT1 = 52 << 20
LIMIT2 = 8 << 20
F32 = jnp.float32
BF16 = jnp.bfloat16


def kv_group(own):
    return 4 if own % 4 == 0 else 1


def silu(v):
    v = v.astype(F32)
    half = 0.5 * v
    return (half + half * jnp.tanh(half)).astype(BF16)


def kernel(nz, nh, docs_hbm, q_hbm, k_hbm, v_hbm, out_ref, scale_ref,
           ends_ref, doc_sem, qb, kb, vb, qa, ka, loc, mask, joinb, keepb, tail, prefix, partial, tin, pin, zin, zout, aout, ain,
           load_sem, ex_send, ex_recv, t_send, t_recv, p_send, p_recv, z_send, z_recv, a_send, a_recv):
    nx = nh // 2
    rows, width = q_hbm.shape
    half = width // 2
    heads = half // DH
    own = heads // nx
    ph = tail.shape[2]
    pieces = own // ph
    docs = ends_ref.shape[0]
    chunk = 2 * rows
    shard = nx * chunk
    longest = nz * shard // nh
    chained = longest > shard
    z = lax.axis_index("ctx")
    h = lax.axis_index("head")
    x = h // 2
    c = h % 2
    o = 1 - c

    def device(xx, cc, zz=None):
        return {"ctx": z if zz is None else zz, "head": 2 * xx + cc}

    ahead = [lax.rem(x + 1 + s, nx) for s in range(nx)]
    behind = [lax.rem(x + nx - 1 - s + nx, nx) for s in range(nx)]

    barrier = pltpu.get_barrier_semaphore()
    pl.semaphore_signal(barrier, inc=1, device_id=device(x, o), device_id_type=MESH)
    for s in range(nx - 1):
        pl.semaphore_signal(barrier, inc=1, device_id=device(ahead[s], c), device_id_type=MESH)

    @pl.when(z > 0)
    def _():
        pl.semaphore_signal(barrier, inc=1, device_id=device(x, c, z - 1), device_id_type=MESH)

    @pl.when(z < nz - 1)
    def _():
        pl.semaphore_signal(barrier, inc=1, device_id=device(x, c, z + 1), device_id_type=MESH)

    docs_copy = pltpu.make_async_copy(docs_hbm, ends_ref, doc_sem)
    docs_copy.start()

    ex = ((k_hbm, kb), (v_hbm, vb), (q_hbm, qb))
    eg = kv_group(own)
    small, large = eg * DH, own * DH
    parts = [(s, j, a) for s in range(nx) for j in range(own // eg) for a in (0, 1)]
    parts += [(s, 0, 2) for s in range(nx)]

    def place(s, j, a):
        size = large if a == 2 else small
        return pl.multiple_of(ahead[s] * large + j * small, small), size

    local_copies = {}

    def start_local(keys):
        for s, j, a in keys:
            at, size = place(s, j, a)
            src, dst = ex[a]
            cp = pltpu.make_async_copy(
                src.at[:, pl.ds(pl.multiple_of(c * half + at, small), size)],
                dst.at[c, :, pl.ds(at, size)], load_sem.at[s, j, a])
            cp.start()
            local_copies[s, j, a] = cp

    start_local([k for k in parts if k[2] != 2])

    pl.semaphore_wait(barrier, nx + jnp.where(z > 0, 1, 0) + jnp.where(z < nz - 1, 1, 0))

    ex_copies = {}

    def start_exchange(keys):
        for s, j, a in keys:
            at, size = place(s, j, a)
            src, dst = ex[a]
            cp = pltpu.make_async_remote_copy(
                src_ref=src.at[:, pl.ds(pl.multiple_of(o * half + at, small), size)],
                dst_ref=dst.at[c, :, pl.ds(at, size)],
                send_sem=ex_send.at[s, j, a], recv_sem=ex_recv.at[s, j, a],
                device_id=device(x, o), device_id_type=MESH)
            cp.start()
            ex_copies[s, j, a] = cp

    start_exchange([k for k in parts if k[2] != 2])

    docs_copy.wait()
    ends = [ends_ref[0]]
    for d in range(1, docs):
        ends.append(ends[-1] + ends_ref[d])

    def seg_of(pos):
        total = jnp.where(pos < 0, -1, 0)
        for end in ends:
            total = total + jnp.where(pos >= end, 1, 0)
        return total

    shard_start = z * (nx * chunk)
    first = shard_start + x * chunk
    row_i = lax.broadcasted_iota(jnp.int32, (chunk, DH), 0)
    seg_r = seg_of(row_i + first)
    col_i = lax.broadcasted_iota(jnp.int32, (8, chunk), 1)
    seg_c = seg_of(col_i + first)
    before = seg_of(first - 1)
    last = seg_of(first + chunk - 1)
    joinb[...] = jnp.where(seg_r == before, 1.0, 0.0)
    keepb[...] = jnp.where(seg_r == last, 1.0, 0.0)
    for g in range(chunk // DH):
        sc = jnp.broadcast_to(seg_c[0:1, g * DH:(g + 1) * DH], (chunk, DH))
        ci = lax.broadcasted_iota(jnp.int32, (chunk, DH), 1) + g * DH
        mask[:, g * DH:(g + 1) * DH] = jnp.where((seg_r == sc) & (row_i >= ci), 1.0, 0.0)
    cont = []
    for xx in range(nx):
        f = shard_start + xx * chunk
        cont.append(jnp.where(seg_of(f - 1) == seg_of(f + chunk - 1), 1.0, 0.0).astype(F32))

    def cols(head):
        return pl.ds(pl.multiple_of(head * DH, DH), DH)

    def take(ref, head):
        return ref[:, :, cols(head)].reshape(chunk, DH)

    t_copies = {}
    for s in range(nx):
        for p in range(pieces):
            for i in range(ph):
                if (p * ph + i) % eg == 0:
                    for a in (0, 1):
                        local_copies[s, (p * ph + i) // eg, a].wait()
                        ex_copies[s, (p * ph + i) // eg, a].wait_recv()
                    if s == 0 and p * ph + i == own - eg:
                        start_local([k for k in parts if k[2] == 2])
                        start_exchange([k for k in parts if k[2] == 2])
                head = ahead[s] * own + p * ph + i
                kk = silu(take(kb, head))
                ka[:, cols(head)] = kk
                masked = (kk.astype(F32) * keepb[...]).astype(BF16)
                t = lax.dot_general(masked, take(vb, head), (((0,), (0,)), ((), ())),
                                    preferred_element_type=F32)
                (tin if s == nx - 1 else tail)[s, p, i] = t.astype(BF16)
            if s < nx - 1:
                cp = pltpu.make_async_remote_copy(
                    src_ref=tail.at[s, p], dst_ref=tin.at[s, p],
                    send_sem=t_send.at[s, p], recv_sem=t_recv.at[s, p],
                    device_id=device(ahead[s], c), device_id_type=MESH)
                cp.start()
                t_copies[s, p] = cp

    for s in range(nx):
        local_copies[s, 0, 2].wait()
        ex_copies[s, 0, 2].wait_recv()

    unroll = 2

    def local_heads(step, carry):
        for i in range(unroll):
            head = step * unroll + i
            qq = silu(take(qb, head))
            qa[:, cols(head)] = qq
            scores = lax.dot_general(qq, ka[:, cols(head)], (((1,), (1,)), ((), ())),
                                     preferred_element_type=F32)
            w = (scores * mask[...]).astype(BF16)
            loc[:, cols(head)] = jnp.dot(w, take(vb, head), preferred_element_type=F32)
        return carry

    steps = heads // unroll
    pre = jnp.minimum(z * 4, steps) if chained else 0
    lax.fori_loop(0, pre, local_heads, 0)

    @pl.when(z == 0)
    def _():
        zin[...] = jnp.zeros_like(zin)

    def z_copy(p):
        return pltpu.make_async_remote_copy(
            src_ref=zout.at[p], dst_ref=zin.at[p], send_sem=z_send.at[p], recv_sem=z_recv.at[p],
            device_id=device(x, c, z + 1), device_id_type=MESH)

    p_copies = {}

    def fold(p):
        for s in range(nx - 1):
            t_copies[s, p].wait_recv()
        add = None
        for xx in range(nx):
            got = tin[lax.rem(x + 2 * nx - 1 - xx, nx), p].astype(F32)
            add = got if xx == 0 else got + add * cont[xx]
            partial[p, xx] = add
        if chained:
            receive(p)
            whole = 1.0
            for xx in range(nx):
                whole = whole * cont[xx]
            add = add + zin[p].astype(F32) * whole
        zout[p] = add.astype(BF16)

        @pl.when(z < nz - 1)
        def _():
            z_copy(p).start()

    def receive(p):
        @pl.when(z > 0)
        def _():
            z_copy(p).wait_recv()

    def spread(p):
        if not chained:
            receive(p)
        carried = zin[p].astype(F32)
        passed = 1.0
        prefix[0, p] = zin[p]
        for xx in range(nx - 1):
            passed = passed * cont[xx]
            prefix[xx + 1, p] = (partial[p, xx] + carried * passed).astype(BF16)
        for s in range(nx - 1):
            cp = pltpu.make_async_remote_copy(
                src_ref=prefix.at[ahead[s], p], dst_ref=pin.at[s, p],
                send_sem=p_send.at[s, p], recv_sem=p_recv.at[s, p],
                device_id=device(ahead[s], c), device_id_type=MESH)
            cp.start()
            p_copies[s, p] = cp

    lag = 0 if chained else min(3, pieces)
    slots = pieces + lag
    for slot in range(slots):
        if slot < pieces:
            fold(slot)
        if slot >= lag:
            spread(slot - lag)
        lax.fori_loop(pre + (steps - pre) * slot // slots, pre + (steps - pre) * (slot + 1) // slots, local_heads, 0)

    a_copies = []
    total = jnp.zeros((rows, DH), F32)

    def finish(head, state):
        inter = jnp.dot(qa[:, cols(head)], state, preferred_element_type=F32)
        att = (loc[:, cols(head)] + inter * joinb[...]).astype(BF16)
        aout[:, :, cols(head)] = att.reshape(2, rows, DH)

    def gather(total, ref, head, side):
        for i in range(ph):
            v = ref[:, cols(head + i)]
            out_ref[:, pl.ds(pl.multiple_of(side * half + (head + i) * DH, DH), DH)] = v
            v = v.astype(F32)
            total = total + v * v
        return total

    late = min(8, heads // ph)
    for s in [nx - 1] + list(range(nx - 1)):
        owner = x if s == nx - 1 else behind[s]
        for p in range(pieces):
            if s < nx - 1:
                p_copies[s, p].wait_recv()
            for i in range(ph):
                state = prefix[x, p, i] if s == nx - 1 else pin[s, p, i]
                finish(owner * own + p * ph + i, state)
            at = pl.ds(pl.multiple_of((owner * own + p * ph) * DH, ph * DH), ph * DH)
            cp = pltpu.make_async_remote_copy(
                src_ref=aout.at[o, :, at], dst_ref=ain.at[:, at],
                send_sem=a_send.at[s, p], recv_sem=a_recv.at[s, p],
                device_id=device(x, o), device_id_type=MESH)
            cp.start()
            a_copies.append((cp, owner * own + p * ph))
            total = gather(total, aout.at[c], owner * own + p * ph, c)
            if len(a_copies) > late:
                done, head = a_copies[-1 - late]
                done.wait_recv()
                total = gather(total, ain, head, o)

    for done, head in a_copies[-late:]:
        done.wait_recv()
        total = gather(total, ain, head, o)
    scale = lax.rsqrt(jnp.sum(total, axis=1, keepdims=True) / width + 1e-05)
    scale_ref[...] = jnp.broadcast_to(scale, (rows, DH))

    for cp in ex_copies.values():
        cp.wait_send()
    for cp in t_copies.values():
        cp.wait_send()
    for cp in p_copies.values():
        cp.wait_send()
    for cp, _ in a_copies:
        cp.wait_send()

    @pl.when(z < nz - 1)
    def _():
        for p in range(pieces):
            z_copy(p).wait_send()


def scale_kernel(parts, att_ref, scale_ref, gain_ref, out_hbm, buf, sems):
    rows, width = att_ref.shape
    part = width // parts
    scale = scale_ref[...]
    copies = []
    for j in range(parts):
        for i in range(part // DH):
            at = j * part + i * DH
            v = att_ref[:, at:at + DH].astype(F32)
            buf[j, :, i * DH:(i + 1) * DH] = (v * scale * gain_ref[0:1, at:at + DH]).astype(BF16)
        cp = pltpu.make_async_copy(buf.at[j], out_hbm.at[:, j * part:(j + 1) * part], sems.at[j])
        cp.start()
        copies.append(cp)
    for cp in copies:
        cp.wait()


def per_device(nz, nh, queries, keys_in, values, doc_lengths, rms_gain):
    rows, width = queries.shape
    nx = nh // 2
    half = width // 2
    heads = half // DH
    own = heads // nx
    ph = 1
    pieces = own // ph
    far = max(nx - 1, 1)
    docs = doc_lengths.shape
    kv = (nx, own // kv_group(own), 3)
    chunk = 2 * rows
    wide = pltpu.VMEM((2, rows, half), BF16)
    flat = pltpu.VMEM((chunk, half), BF16)
    dma = pltpu.SemaphoreType.DMA
    hbm_spec = pl.BlockSpec(memory_space=pltpu.HBM)
    vmem_spec = pl.BlockSpec(memory_space=pltpu.VMEM)
    attended, scale = pl.pallas_call(
        functools.partial(kernel, nz, nh),
        out_shape=(jax.ShapeDtypeStruct((rows, width), BF16), jax.ShapeDtypeStruct((rows, DH), F32)),
        in_specs=[hbm_spec] * 4,
        out_specs=(vmem_spec, vmem_spec),
        scratch_shapes=[
            pltpu.SMEM(docs, jnp.int32), dma(()),
            wide, wide, wide, flat, flat,
            pltpu.VMEM((chunk, half), F32),
            pltpu.VMEM((chunk, chunk), F32),
            pltpu.VMEM((chunk, DH), F32),
            pltpu.VMEM((chunk, DH), F32),
            pltpu.VMEM((far, pieces, ph, DH, DH), BF16),
            pltpu.VMEM((nx, pieces, ph, DH, DH), BF16),
            pltpu.VMEM((pieces, nx, ph, DH, DH), F32),
            pltpu.VMEM((nx, pieces, ph, DH, DH), BF16),
            pltpu.VMEM((far, pieces, ph, DH, DH), BF16),
            pltpu.VMEM((pieces, ph, DH, DH), BF16),
            pltpu.VMEM((pieces, ph, DH, DH), BF16),
            wide,
            pltpu.VMEM((rows, half), BF16),
            dma(kv), dma(kv), dma(kv),
            dma((far, pieces)), dma((far, pieces)),
            dma((far, pieces)), dma((far, pieces)),
            dma((pieces,)), dma((pieces,)),
            dma((nx, pieces)), dma((nx, pieces)),
        ],
        compiler_params=pltpu.CompilerParams(collective_id=0, has_side_effects=True, vmem_limit_bytes=LIMIT1),
        name="scan_attention",
    )(pltpu.with_memory_space_constraint(doc_lengths, pltpu.HBM), queries, keys_in, values)
    parts = 4
    return pl.pallas_call(
        functools.partial(scale_kernel, parts),
        out_shape=jax.ShapeDtypeStruct((rows, width), BF16),
        in_specs=[pl.BlockSpec(memory_space=pltpu.VMEM)] * 3,
        out_specs=pl.BlockSpec(memory_space=pl.ANY),
        scratch_shapes=[pltpu.VMEM((parts, rows, width // parts), BF16), dma((parts,))],
        compiler_params=pltpu.CompilerParams(vmem_limit_bytes=LIMIT2),
        name="scale_rows",
    )(attended, scale, rms_gain.reshape(1, width))


def solution(mesh):
    split = P(("groups", "ctx", "head"), None)
    return jax.shard_map(
        functools.partial(per_device, mesh.shape["ctx"], mesh.shape["head"]),
        mesh=mesh,
        in_specs=(split, split, split, P("groups"), P()),
        out_specs=split,
        check_vma=False,
    )
```

```python
import functools

import jax
import jax.numpy as jnp
from jax import lax
from jax.experimental import pallas as pl
from jax.experimental.pallas import tpu as pltpu
from jax.sharding import PartitionSpec as P

DH = 128
MESH = pl.DeviceIdType.MESH
LIMIT1 = 52 << 20
LIMIT2 = 8 << 20
F32 = jnp.float32
BF16 = jnp.bfloat16
BATCH = 4


def silu(v):
    v = v.astype(F32)
    half = 0.5 * v
    return (half + half * jnp.tanh(half)).astype(BF16)


def kernel(nz, nh, group, docs_hbm, q_hbm, k_hbm, v_hbm, out_ref, scale_ref,
           ends_ref, doc_sem, qb, kb, vb, wq, maskb, joinb, keepb, tsend, tt, xout, tin, partial, zin, zout, prefix, pin, st, fin,
           load_sem, s_send, s_recv, t_send, t_recv, z_send, z_recv, p_send, p_recv, f_send, f_recv):
    nx = nh // 2
    rows, width = q_hbm.shape
    heads = width // DH
    half = heads // 2
    own = half // nx
    docs = ends_ref.shape[0]
    chunk = 2 * rows
    shard = nx * chunk
    longest = nz * shard // nh
    chained = longest > shard
    z = lax.axis_index("ctx")
    h = lax.axis_index("head")
    x = h // 2
    c = h % 2
    o = 1 - c

    def device(xx, cc, zz=None):
        return {"ctx": z if zz is None else zz, "head": 2 * xx + cc}

    ahead = [lax.rem(x + 1 + s, nx) for s in range(nx)]
    behind = [lax.rem(x + 2 * nx - 1 - s, nx) for s in range(nx)]

    barrier = pltpu.get_barrier_semaphore()
    pl.semaphore_signal(barrier, inc=1, device_id=device(x, o), device_id_type=MESH)
    for s in range(nx - 1):
        pl.semaphore_signal(barrier, inc=1, device_id=device(ahead[s], c), device_id_type=MESH)

    @pl.when(z > 0)
    def _():
        pl.semaphore_signal(barrier, inc=1, device_id=device(x, c, z - 1), device_id_type=MESH)

    @pl.when(z < nz - 1)
    def _():
        pl.semaphore_signal(barrier, inc=1, device_id=device(x, c, z + 1), device_id_type=MESH)

    docs_copy = pltpu.make_async_copy(docs_hbm, ends_ref, doc_sem)
    docs_copy.start()

    def cols(head, count=1):
        return pl.ds(pl.multiple_of(head * DH, DH), count * DH)

    def first_head(side, s, g):
        return (o if side else c) * half + ahead[s] * own + g * group

    groups = own // group

    def load(side, s, g, count, sem):
        at = cols(first_head(side, s, g), count)
        for src, dst in ((k_hbm, kb), (v_hbm, vb)):
            pltpu.make_async_copy(src.at[:, at], dst.at[:, at], load_sem.at[sem]).start()

    def loaded(sem, count):
        at = pl.ds(0, 4 * count * DH)
        pltpu.make_async_copy(k_hbm.at[:, at], kb.at[:, at], load_sem.at[sem]).wait()

    for side in (1, 0):
        load(side, 0, 0, group, 0)
    for s in range(nx):
        skip = 0 if s else 1
        if groups > skip:
            for side in (1, 0):
                load(side, s, skip, own - skip * group, s + 1)
    q_copy = pltpu.make_async_copy(q_hbm, qb, load_sem.at[nx + 1])
    q_copy.start()

    docs_copy.wait()
    ends = [ends_ref[0]]
    for d in range(1, docs):
        ends.append(ends[-1] + ends_ref[d])

    def seg_of(pos):
        total = jnp.where(pos < 0, -1, 0)
        for end in ends:
            total = total + jnp.where(pos >= end, 1, 0)
        return total

    def spans(start, count):
        return jnp.where(seg_of(start - 1) == seg_of(start + count - 1), 1.0, 0.0).astype(F32)

    shard_start = z * shard
    chip = shard_start + x * chunk
    first = chip + c * rows
    row_i = lax.broadcasted_iota(jnp.int32, (rows, DH), 0)
    seg_r = seg_of(row_i + first)
    joinb[...] = jnp.where(seg_r == seg_of(first - 1), 1.0, 0.0).astype(BF16)
    keepb[...] = jnp.where(seg_r == seg_of(first + rows - 1), 1.0, 0.0).astype(BF16)
    col_i = lax.broadcasted_iota(jnp.int32, (8, rows), 1)
    seg_c = seg_of(col_i + first)[0:1]
    for g in range(rows // DH):
        sc = jnp.broadcast_to(seg_c[:, g * DH:(g + 1) * DH], (rows, DH))
        ci = lax.broadcasted_iota(jnp.int32, (rows, DH), 1) + g * DH
        maskb[:, g * DH:(g + 1) * DH] = jnp.where((seg_r == sc) & (row_i >= ci), 1.0, 0.0).astype(BF16)
    low = spans(chip, rows)
    high = spans(chip + rows, rows)
    cont = [spans(shard_start + xx * chunk, chunk) for xx in range(nx)]

    def tails(s, g):
        if s == 0 and g == 0:
            loaded(0, group)
        elif s == 0 and g == 1:
            loaded(1, own - group)
        elif g == 0:
            loaded(s + 1, own)
        for i in range(group):
            for side in (1, 0):
                at = cols(first_head(side, s, g) + i)
                kk = silu(kb[:, at])
                kb[:, at] = kk
                t = lax.dot_general(kk * keepb[...], vb[:, at], (((0,), (0,)), ((), ())), preferred_element_type=F32).astype(BF16)
                if side:
                    tsend[s, g * group + i] = t
                else:
                    tt[c, s, g * group + i] = t

    s_copies = {}

    def pass_tails(s, g):
        at = pl.ds(g * group, group)
        cp = pltpu.make_async_remote_copy(
            src_ref=tsend.at[s, at], dst_ref=tt.at[c, s, at], send_sem=s_send, recv_sem=s_recv.at[s, g],
            device_id=device(x, o), device_id_type=MESH)
        cp.start()
        s_copies[s, g] = cp

    t_copies = {}

    def join_tails(s, g):
        s_copies[s, g].wait_recv()
        for i in range(group):
            p = g * group + i
            t = (tt[1, s, p].astype(F32) + tt[0, s, p].astype(F32) * high).astype(BF16)
            if s == nx - 1:
                tin[s, p] = t
                continue
            xout[s, p] = t
            cp = pltpu.make_async_remote_copy(
                src_ref=xout.at[s, p], dst_ref=tin.at[s, p], send_sem=t_send, recv_sem=t_recv.at[s, p],
                device_id=device(ahead[s], c), device_id_type=MESH)
            cp.start()
            t_copies[s, p] = cp

    tails(0, 0)
    pl.semaphore_wait(barrier, nx + jnp.where(z > 0, 1, 0) + jnp.where(z < nz - 1, 1, 0))
    pass_tails(0, 0)
    order = [(s, g) for s in range(nx) for g in range(groups)]
    delay = min(3, len(order) - 1)
    for n, (s, g) in enumerate(order):
        if n:
            tails(s, g)
            pass_tails(s, g)
        if n >= delay:
            join_tails(*order[n - delay])
    for s, g in order[len(order) - delay:]:
        join_tails(s, g)

    q_copy.wait()

    def head_of(side, s, p):
        owner = x if s == nx - 1 else behind[s]
        return (o if side else c) * half + owner * own + p

    def local(batch):
        for one in batch:
            head = head_of(*one)
            qq = silu(qb[:, cols(head)])
            scores = lax.dot_general(qq, kb[:, cols(head)], (((1,), (1,)), ((), ())), preferred_element_type=F32)
            wq[head, :, :rows] = scores.astype(BF16) * maskb[...]
            wq[head, :, rows:] = qq * joinb[...]

    @pl.when(z == 0)
    def _():
        zin[...] = jnp.zeros_like(zin)

    def z_copy(p):
        return pltpu.make_async_remote_copy(
            src_ref=zout.at[p], dst_ref=zin.at[p], send_sem=z_send, recv_sem=z_recv.at[p],
            device_id=device(x, c, z + 1), device_id_type=MESH)

    def receive(p):
        @pl.when(z > 0)
        def _():
            z_copy(p).wait_recv()

    def fold(p):
        for s in range(nx - 1):
            t_copies[s, p].wait_recv()
        add = None
        for xx in range(nx):
            got = tin[lax.rem(x + 2 * nx - 1 - xx, nx), p].astype(F32)
            add = got if xx == 0 else got + add * cont[xx]
            partial[p, xx] = add
        if chained:
            receive(p)
            whole = 1.0
            for xx in range(nx):
                whole = whole * cont[xx]
            add = add + zin[p].astype(F32) * whole
        zout[p] = add.astype(BF16)

        @pl.when(z < nz - 1)
        def _():
            z_copy(p).start()

    p_copies = {}
    f_copies = {}

    def forward(s, p, state):
        into = tt[0, nx - 1 if s == nx - 1 else nx - 2 - s, p].astype(F32) + state.astype(F32) * low
        st[0, s, p] = state
        st[1, s, p] = into.astype(BF16)
        cp = pltpu.make_async_remote_copy(
            src_ref=st.at[o, s, p], dst_ref=fin.at[s, p], send_sem=f_send, recv_sem=f_recv.at[s, p],
            device_id=device(x, o), device_id_type=MESH)
        cp.start()
        f_copies[s, p] = cp

    def spread(p):
        if not chained:
            receive(p)
        carried = zin[p].astype(F32)
        passed = 1.0
        prefix[0, p] = zin[p]
        for xx in range(nx - 1):
            passed = passed * cont[xx]
            prefix[xx + 1, p] = (partial[p, xx] + carried * passed).astype(BF16)
        for s in range(nx - 1):
            cp = pltpu.make_async_remote_copy(
                src_ref=prefix.at[ahead[s], p], dst_ref=pin.at[s, p],
                send_sem=p_send, recv_sem=p_recv.at[s, p],
                device_id=device(ahead[s], c), device_id_type=MESH)
            cp.start()
            p_copies[s, p] = cp
        forward(nx - 1, p, prefix[x, p])

    def finish(batch, total):
        for side, s, p in batch:
            if side:
                f_copies[s, p].wait_recv()
        for side, s, p in batch:
            head = head_of(side, s, p)
            state = fin[s, p] if side else st[c, s, p]
            both = jnp.concatenate([vb[:, cols(head)], state], axis=0)
            att = jnp.dot(wq[head], both, preferred_element_type=F32).astype(BF16)
            out_ref[:, cols(head)] = att
            att = att.astype(F32)
            total = total + att * att
        return total

    lag = 0 if chained else min(3, own)
    rest = [(s, p) for s in range(nx - 1) for p in range(own)]
    every = [(side, s, p) for s, p in [(nx - 1, p) for p in range(own)] + rest for side in (0, 1)]
    ready = {}
    for n in range(own):
        ready[0, nx - 1, n] = n + lag
        ready[1, nx - 1, n] = n + lag + 2
    for n, (s, p) in enumerate(rest):
        ready[0, s, p] = n + own
        ready[1, s, p] = n + own + 2
    slots = own + len(rest)
    waiting = sorted(ready, key=lambda one: (ready[one], one))
    todo = list(every)
    total = jnp.zeros((rows, DH), F32)
    for slot in range(slots):
        if slot < own:
            fold(slot)
        if lag <= slot < own + lag:
            spread(slot - lag)
        if slot >= own:
            s, p = rest[slot - own]
            p_copies[s, p].wait_recv()
            forward(s, p, pin[s, p])
        count = -(-len(todo) // max(own - slot, 1))
        local(todo[:count])
        todo = todo[count:]
        now = [one for one in waiting if ready[one] <= slot and one not in todo]
        if len(now) >= BATCH:
            total = finish(now[:BATCH], total)
            waiting = [one for one in waiting if one not in now[:BATCH]]
    while waiting:
        total = finish(waiting[:2], total)
        waiting = waiting[2:]
    scale = lax.rsqrt(jnp.sum(total, axis=1, keepdims=True) / width + 1e-05)
    scale_ref[...] = jnp.broadcast_to(scale, (rows, DH))

    def sent(src, dst, sem, recv):
        pltpu.make_async_remote_copy(
            src_ref=src, dst_ref=dst, send_sem=sem, recv_sem=recv,
            device_id=device(x, o), device_id_type=MESH).wait_send()

    sent(tsend, tt.at[c], s_send, s_recv.at[0, 0])
    if nx > 1:
        sent(xout, xout, t_send, t_recv.at[0, 0])
        sent(pin, pin, p_send, p_recv.at[0, 0])
    sent(st.at[o], fin, f_send, f_recv.at[0, 0])

    @pl.when(z < nz - 1)
    def _():
        sent(zout, zin, z_send, z_recv.at[0])


def scale_kernel(parts, att_ref, scale_ref, gain_ref, out_hbm, buf, sems):
    rows, width = att_ref.shape
    part = width // parts
    scale = scale_ref[...]
    copies = []
    for j in range(parts):
        for i in range(part // DH):
            at = j * part + i * DH
            v = att_ref[:, at:at + DH].astype(F32)
            buf[j, :, i * DH:(i + 1) * DH] = (v * scale * gain_ref[0:1, at:at + DH]).astype(BF16)
        cp = pltpu.make_async_copy(buf.at[j], out_hbm.at[:, j * part:(j + 1) * part], sems.at[j])
        cp.start()
        copies.append(cp)
    for cp in copies:
        cp.wait()


def per_device(nz, nh, queries, keys_in, values, doc_lengths, rms_gain):
    rows, width = queries.shape
    nx = nh // 2
    heads = width // DH
    own = heads // 2 // nx
    group = 2 if own % 2 == 0 else 1
    groups = own // group
    far = max(nx - 1, 1)
    docs = doc_lengths.shape
    vmem = pltpu.VMEM
    full = vmem((rows, width), BF16)
    dma = pltpu.SemaphoreType.DMA
    hbm_spec = pl.BlockSpec(memory_space=pltpu.HBM)
    vmem_spec = pl.BlockSpec(memory_space=pltpu.VMEM)
    attended, scale = pl.pallas_call(
        functools.partial(kernel, nz, nh, group),
        out_shape=(jax.ShapeDtypeStruct((rows, width), BF16), jax.ShapeDtypeStruct((rows, DH), F32)),
        in_specs=[hbm_spec] * 4,
        out_specs=(vmem_spec, vmem_spec),
        scratch_shapes=[
            pltpu.SMEM(docs, jnp.int32), dma(()),
            full, full, full,
            vmem((heads, rows, rows + DH), BF16),
            vmem((rows, rows), BF16),
            vmem((rows, DH), BF16),
            vmem((rows, DH), BF16),
            vmem((nx, own, DH, DH), BF16),
            vmem((2, nx, own, DH, DH), BF16),
            vmem((far, own, DH, DH), BF16),
            vmem((nx, own, DH, DH), BF16),
            vmem((own, nx, DH, DH), F32),
            vmem((own, DH, DH), BF16),
            vmem((own, DH, DH), BF16),
            vmem((nx, own, DH, DH), BF16),
            vmem((far, own, DH, DH), BF16),
            vmem((2, nx, own, DH, DH), BF16),
            vmem((nx, own, DH, DH), BF16),
            dma((nx + 2,)),
            dma(()), dma((nx, groups)),
            dma(()), dma((far, own)),
            dma(()), dma((own,)),
            dma(()), dma((far, own)),
            dma(()), dma((nx, own)),
        ],
        compiler_params=pltpu.CompilerParams(collective_id=0, has_side_effects=True, vmem_limit_bytes=LIMIT1),
        name="scan_attention",
    )(pltpu.with_memory_space_constraint(doc_lengths, pltpu.HBM), queries, keys_in, values)
    parts = 4
    return pl.pallas_call(
        functools.partial(scale_kernel, parts),
        out_shape=jax.ShapeDtypeStruct((rows, width), BF16),
        in_specs=[pl.BlockSpec(memory_space=pltpu.VMEM)] * 3,
        out_specs=pl.BlockSpec(memory_space=pl.ANY),
        scratch_shapes=[pltpu.VMEM((parts, rows, width // parts), BF16), dma((parts,))],
        compiler_params=pltpu.CompilerParams(vmem_limit_bytes=LIMIT2),
        name="scale_rows",
    )(attended, scale, rms_gain.reshape(1, width))


def solution(mesh):
    split = P(("groups", "ctx", "head"), None)
    return jax.shard_map(
        functools.partial(per_device, mesh.shape["ctx"], mesh.shape["head"]),
        mesh=mesh,
        in_specs=(split, split, split, P("groups"), P()),
        out_specs=split,
        check_vma=False,
    )
```

```python
import functools

import jax
import jax.numpy as jnp
from jax import lax
from jax.experimental import pallas as pl
from jax.experimental.pallas import tpu as pltpu
from jax.sharding import PartitionSpec as P

DH = 128
MESH = pl.DeviceIdType.MESH
LIMIT1 = 52 << 20
LIMIT2 = 8 << 20
F32 = jnp.float32
BF16 = jnp.bfloat16
BATCH = 4


def silu(v):
    v = v.astype(F32)
    half = 0.5 * v
    return (half + half * jnp.tanh(half)).astype(BF16)


def kernel(nz, nh, group, docs_hbm, q_hbm, k_hbm, v_hbm, out_ref, scale_ref,
           ends_ref, doc_sem, qb, kb, vb, wq, maskb, joinb, keepb, tsend, tt, xout, tin, partial, zin, zout, prefix, pin, st, fin, early,
           load_sem, s_send, s_recv, t_send, t_recv, z_send, z_recv, p_send, p_recv, f_send, f_recv, e_send, e_recv):
    nx = nh // 2
    rows, width = q_hbm.shape
    heads = width // DH
    half = heads // 2
    own = half // nx
    docs = ends_ref.shape[0]
    chunk = 2 * rows
    shard = nx * chunk
    longest = nz * shard // nh
    chained = longest > shard
    z = lax.axis_index("ctx")
    h = lax.axis_index("head")
    x = h // 2
    c = h % 2
    o = 1 - c

    def device(xx, cc, zz=None):
        return {"ctx": z if zz is None else zz, "head": 2 * xx + cc}

    ahead = [lax.rem(x + 1 + s, nx) for s in range(nx)]
    behind = [lax.rem(x + 2 * nx - 1 - s, nx) for s in range(nx)]

    barrier = pltpu.get_barrier_semaphore()
    pl.semaphore_signal(barrier, inc=1, device_id=device(x, o), device_id_type=MESH)
    for s in range(nx - 1):
        pl.semaphore_signal(barrier, inc=1, device_id=device(ahead[s], c), device_id_type=MESH)

    across = [ahead[0], behind[0]][:min(nx - 1, 2)]
    for xx in across:
        pl.semaphore_signal(barrier, inc=1, device_id=device(xx, o), device_id_type=MESH)

    @pl.when(z > 0)
    def _():
        pl.semaphore_signal(barrier, inc=1, device_id=device(x, c, z - 1), device_id_type=MESH)

    @pl.when(z < nz - 1)
    def _():
        pl.semaphore_signal(barrier, inc=1, device_id=device(x, c, z + 1), device_id_type=MESH)

    def cols(head, count=1):
        return pl.ds(pl.multiple_of(head * DH, DH), count * DH)

    def first_head(side, s, g):
        return (o if side else c) * half + ahead[s] * own + g * group

    groups = own // group

    def load(side, s, g, count, sem):
        at = cols(first_head(side, s, g), count)
        for src, dst in ((k_hbm, kb), (v_hbm, vb)):
            pltpu.make_async_copy(src.at[:, at], dst.at[:, at], load_sem.at[sem]).start()

    def loaded(sem, count):
        at = pl.ds(0, 4 * count * DH)
        pltpu.make_async_copy(k_hbm.at[:, at], kb.at[:, at], load_sem.at[sem]).wait()

    for side in (1, 0):
        load(side, 0, 0, group, 0)
    docs_copy = pltpu.make_async_copy(docs_hbm, ends_ref, doc_sem)
    docs_copy.start()
    for s in range(nx):
        skip = 0 if s else 1
        if groups > skip:
            for side in (1, 0):
                load(side, s, skip, own - skip * group, s + 1)
    q_copy = pltpu.make_async_copy(q_hbm, qb, load_sem.at[nx + 1])
    q_copy.start()

    def activate(s, g):
        for i in range(group):
            for side in (1, 0):
                at = cols(first_head(side, s, g) + i)
                kb[:, at] = silu(kb[:, at])

    loaded(0, group)
    activate(0, 0)
    docs_copy.wait()
    ends = [ends_ref[0]]
    for d in range(1, docs):
        ends.append(ends[-1] + ends_ref[d])

    def seg_of(pos):
        total = jnp.where(pos < 0, -1, 0)
        for end in ends:
            total = total + jnp.where(pos >= end, 1, 0)
        return total

    def spans(start, count):
        return jnp.where(seg_of(start - 1) == seg_of(start + count - 1), 1.0, 0.0).astype(F32)

    shard_start = z * shard
    chip = shard_start + x * chunk
    first = chip + c * rows
    row_i = lax.broadcasted_iota(jnp.int32, (rows, DH), 0)
    seg_r = seg_of(row_i + first)
    joinb[...] = jnp.where(seg_r == seg_of(first - 1), 1.0, 0.0).astype(BF16)
    keepb[...] = jnp.where(seg_r == seg_of(first + rows - 1), 1.0, 0.0).astype(BF16)
    col_i = lax.broadcasted_iota(jnp.int32, (8, rows), 1)
    seg_c = seg_of(col_i + first)[0:1]
    for g in range(rows // DH):
        sc = jnp.broadcast_to(seg_c[:, g * DH:(g + 1) * DH], (rows, DH))
        ci = lax.broadcasted_iota(jnp.int32, (rows, DH), 1) + g * DH
        maskb[:, g * DH:(g + 1) * DH] = jnp.where((seg_r == sc) & (row_i >= ci), 1.0, 0.0).astype(BF16)
    low = spans(chip, rows)
    high = spans(chip + rows, rows)
    other = spans(shard_start + behind[0] * chunk + rows, rows)
    cont = [spans(shard_start + xx * chunk, chunk) for xx in range(nx)]

    def tails(s, g):
        if s == 0 and g == 1:
            loaded(1, own - group)
        elif s and g == 0:
            loaded(s + 1, own)
        for i in range(group):
            for side in (1, 0):
                at = cols(first_head(side, s, g) + i)
                kk = kb[:, at] if s == 0 and g == 0 else silu(kb[:, at])
                kb[:, at] = kk
                t = lax.dot_general(kk * keepb[...], vb[:, at], (((0,), (0,)), ((), ())), preferred_element_type=F32).astype(BF16)
                if side:
                    tsend[s, g * group + i] = t
                else:
                    tt[c, s, g * group + i] = t

    s_copies = {}

    def pass_tails(s, g):
        at = pl.ds(g * group, group)
        cp = pltpu.make_async_remote_copy(
            src_ref=tsend.at[s, at], dst_ref=tt.at[c, s, at], send_sem=s_send, recv_sem=s_recv.at[s, g],
            device_id=device(x, o), device_id_type=MESH)
        cp.start()
        s_copies[s, g] = cp

    t_copies = {}

    def join_tails(s, g):
        s_copies[s, g].wait_recv()
        for i in range(group):
            p = g * group + i
            if s == 0 and p == 0 and nx > 1:
                continue
            t = (tt[1, s, p].astype(F32) + tt[0, s, p].astype(F32) * high).astype(BF16)
            if s == nx - 1:
                tin[s, p] = t
                continue
            xout[s * own + p] = t
            cp = pltpu.make_async_remote_copy(
                src_ref=xout.at[s * own + p], dst_ref=tin.at[s, p], send_sem=t_send, recv_sem=t_recv.at[s, p],
                device_id=device(ahead[s], c), device_id_type=MESH)
            cp.start()
            t_copies[s, p] = cp

    tails(0, 0)
    pl.semaphore_wait(barrier, nx + len(across) + jnp.where(z > 0, 1, 0) + jnp.where(z < nz - 1, 1, 0))
    e_copies = []
    if nx > 1:
        for n, (src, cc) in enumerate(((tt.at[c, 0, 0], c), (tsend.at[0, 0], o))):
            cp = pltpu.make_async_remote_copy(
                src_ref=src, dst_ref=early.at[c], send_sem=e_send, recv_sem=e_recv.at[n],
                device_id=device(ahead[0], cc), device_id_type=MESH)
            cp.start()
            e_copies.append(cp)
    pass_tails(0, 0)
    order = [(s, g) for s in range(nx) for g in range(groups)]
    delay = min(3, len(order) - 1)
    for n, (s, g) in enumerate(order):
        if n:
            tails(s, g)
            pass_tails(s, g)
        if n >= delay:
            join_tails(*order[n - delay])
    for s, g in order[len(order) - delay:]:
        join_tails(s, g)

    q_copy.wait()

    def head_of(side, s, p):
        owner = x if s == nx - 1 else behind[s]
        return (o if side else c) * half + owner * own + p

    def local(batch):
        for one in batch:
            head = head_of(*one)
            qq = silu(qb[:, cols(head)])
            scores = lax.dot_general(qq, kb[:, cols(head)], (((1,), (1,)), ((), ())), preferred_element_type=F32)
            wq[head, :, :rows] = scores.astype(BF16) * maskb[...]
            wq[head, :, rows:] = qq * joinb[...]

    @pl.when(z == 0)
    def _():
        zin[...] = jnp.zeros_like(zin)

    @pl.when((z == 0) & (x == 0))
    def _():
        pin[...] = jnp.zeros_like(pin)

    def z_copy(p):
        return pltpu.make_async_remote_copy(
            src_ref=zout.at[p], dst_ref=zin.at[p], send_sem=z_send, recv_sem=z_recv.at[p],
            device_id=device(x, c, z + 1), device_id_type=MESH)

    def receive(p):
        @pl.when(z > 0)
        def _():
            z_copy(p).wait_recv()

    def fold(p):
        for s in range(nx - 1):
            if s == 0 and p == 0:
                for cp in e_copies:
                    cp.wait_recv()
                tin[0, 0] = (early[1].astype(F32) + early[0].astype(F32) * other).astype(BF16)
                continue
            t_copies[s, p].wait_recv()
        add = None
        for xx in range(nx):
            got = tin[lax.rem(x + 2 * nx - 1 - xx, nx), p].astype(F32)
            add = got if xx == 0 else got + add * cont[xx]
            partial[p, xx] = add
        if chained:
            receive(p)
            whole = 1.0
            for xx in range(nx):
                whole = whole * cont[xx]
            add = add + zin[p].astype(F32) * whole
        zout[p] = add.astype(BF16)

        @pl.when(z < nz - 1)
        def _():
            z_copy(p).start()

    p_copies = {}
    f_copies = {}

    def forward(s, p, state):
        into = tt[0, nx - 1 if s == nx - 1 else nx - 2 - s, p].astype(F32) + state.astype(F32) * low
        st[0, s, p] = state
        st[1, s, p] = into.astype(BF16)
        cp = pltpu.make_async_remote_copy(
            src_ref=st.at[o, s, p], dst_ref=fin.at[s, p], send_sem=f_send, recv_sem=f_recv.at[s, p],
            device_id=device(x, o), device_id_type=MESH)
        cp.start()
        f_copies[s, p] = cp

    def spread(p):
        if not chained:
            receive(p)
        carried = zin[p].astype(F32)
        passed = 1.0
        prefix[0, p] = zin[p]
        for xx in range(nx - 1):
            passed = passed * cont[xx]
            prefix[xx + 1, p] = (partial[p, xx] + carried * passed).astype(BF16)
        for s in range(nx - 1):
            cp = pltpu.make_async_remote_copy(
                src_ref=prefix.at[ahead[s], p], dst_ref=pin.at[s * own + p],
                send_sem=p_send, recv_sem=p_recv.at[s, p],
                device_id=device(ahead[s], c), device_id_type=MESH)
            pl.when((z > 0) | (ahead[s] > 0))(cp.start)
            p_copies[s, p] = cp
        forward(nx - 1, p, prefix[x, p])

    def finish(batch, total):
        for side, s, p in batch:
            if side:
                f_copies[s, p].wait_recv()
        for side, s, p in batch:
            head = head_of(side, s, p)
            state = fin[s, p] if side else st[c, s, p]
            both = jnp.concatenate([vb[:, cols(head)], state], axis=0)
            att = jnp.dot(wq[head], both, preferred_element_type=F32).astype(BF16)
            out_ref[:, cols(head)] = att
            att = att.astype(F32)
            total = total + att * att
        return total

    lag = 0 if chained else min(3, own)
    rest = [(s, p) for s in range(nx - 1) for p in range(own)]
    every = [(side, s, p) for s, p in [(nx - 1, p) for p in range(own)] + rest for side in (0, 1)]
    ready = {}
    for n in range(own):
        ready[0, nx - 1, n] = n + lag
        ready[1, nx - 1, n] = n + lag + 2
    for n, (s, p) in enumerate(rest):
        ready[0, s, p] = n + own
        ready[1, s, p] = n + own + 2
    slots = own + len(rest)
    waiting = sorted(ready, key=lambda one: (ready[one], one))
    todo = list(every)
    total = jnp.zeros((rows, DH), F32)
    for slot in range(slots):
        if slot < own:
            fold(slot)
        if lag <= slot < own + lag:
            spread(slot - lag)
        if slot >= own:
            s, p = rest[slot - own]
            pl.when((z > 0) | (x > 0))(p_copies[s, p].wait_recv)
            forward(s, p, pin[s * own + p])
        count = -(-len(todo) // max(own - slot, 1))
        local(todo[:count])
        todo = todo[count:]
        now = [one for one in waiting if ready[one] <= slot and one not in todo]
        if len(now) >= BATCH:
            total = finish(now[:BATCH], total)
            waiting = [one for one in waiting if one not in now[:BATCH]]
    while waiting:
        total = finish(waiting[:2], total)
        waiting = waiting[2:]
    scale = lax.rsqrt(jnp.sum(total, axis=1, keepdims=True) / width + 1e-05)
    scale_ref[...] = jnp.broadcast_to(scale, (rows, DH))

    def sent(src, dst, sem, recv):
        pltpu.make_async_remote_copy(
            src_ref=src, dst_ref=dst, send_sem=sem, recv_sem=recv,
            device_id=device(x, o), device_id_type=MESH).wait_send()

    sent(tsend, tt.at[c], s_send, s_recv.at[0, 0])
    if nx > 1:
        sent(early, early, e_send, e_recv.at[0])
        late = pl.ds(1, (nx - 1) * own - 1)
        sent(xout.at[late], xout.at[late], t_send, t_recv.at[0, 0])

        @pl.when((z > 0) | (x == 0))
        def _():
            sent(pin, pin, p_send, p_recv.at[0, 0])

    if nx > 2:
        @pl.when((z == 0) & (x > 0))
        def _():
            most = pl.ds(0, (nx - 2) * own)
            sent(pin.at[most], pin.at[most], p_send, p_recv.at[0, 0])

    sent(st.at[o], fin, f_send, f_recv.at[0, 0])

    @pl.when(z < nz - 1)
    def _():
        sent(zout, zin, z_send, z_recv.at[0])


def scale_kernel(parts, att_ref, scale_ref, gain_ref, out_hbm, buf, sems):
    rows, width = att_ref.shape
    part = width // parts
    scale = scale_ref[...]
    copies = []
    for j in range(parts):
        for i in range(part // DH):
            at = j * part + i * DH
            v = att_ref[:, at:at + DH].astype(F32)
            buf[j, :, i * DH:(i + 1) * DH] = (v * scale * gain_ref[0:1, at:at + DH]).astype(BF16)
        cp = pltpu.make_async_copy(buf.at[j], out_hbm.at[:, j * part:(j + 1) * part], sems.at[j])
        cp.start()
        copies.append(cp)
    for cp in copies:
        cp.wait()


def per_device(nz, nh, queries, keys_in, values, doc_lengths, rms_gain):
    rows, width = queries.shape
    nx = nh // 2
    heads = width // DH
    own = heads // 2 // nx
    group = 2 if own % 2 == 0 else 1
    groups = own // group
    far = max(nx - 1, 1)
    docs = doc_lengths.shape
    vmem = pltpu.VMEM
    full = vmem((rows, width), BF16)
    dma = pltpu.SemaphoreType.DMA
    hbm_spec = pl.BlockSpec(memory_space=pltpu.HBM)
    vmem_spec = pl.BlockSpec(memory_space=pltpu.VMEM)
    attended, scale = pl.pallas_call(
        functools.partial(kernel, nz, nh, group),
        out_shape=(jax.ShapeDtypeStruct((rows, width), BF16), jax.ShapeDtypeStruct((rows, DH), F32)),
        in_specs=[hbm_spec] * 4,
        out_specs=(vmem_spec, vmem_spec),
        scratch_shapes=[
            pltpu.SMEM(docs, jnp.int32), dma(()),
            full, full, full,
            vmem((heads, rows, rows + DH), BF16),
            vmem((rows, rows), BF16),
            vmem((rows, DH), BF16),
            vmem((rows, DH), BF16),
            vmem((nx, own, DH, DH), BF16),
            vmem((2, nx, own, DH, DH), BF16),
            vmem((far * own, DH, DH), BF16),
            vmem((nx, own, DH, DH), BF16),
            vmem((own, nx, DH, DH), F32),
            vmem((own, DH, DH), BF16),
            vmem((own, DH, DH), BF16),
            vmem((nx, own, DH, DH), BF16),
            vmem((far * own, DH, DH), BF16),
            vmem((2, nx, own, DH, DH), BF16),
            vmem((nx, own, DH, DH), BF16),
            vmem((2, DH, DH), BF16),
            dma((nx + 2,)),
            dma(()), dma((nx, groups)),
            dma(()), dma((far, own)),
            dma(()), dma((own,)),
            dma(()), dma((far, own)),
            dma(()), dma((nx, own)),
            dma(()), dma((2,)),
        ],
        compiler_params=pltpu.CompilerParams(collective_id=0, has_side_effects=True, vmem_limit_bytes=LIMIT1),
        name="scan_attention",
    )(pltpu.with_memory_space_constraint(doc_lengths, pltpu.HBM), queries, keys_in, values)
    parts = 4
    return pl.pallas_call(
        functools.partial(scale_kernel, parts),
        out_shape=jax.ShapeDtypeStruct((rows, width), BF16),
        in_specs=[pl.BlockSpec(memory_space=pltpu.VMEM)] * 3,
        out_specs=pl.BlockSpec(memory_space=pl.ANY),
        scratch_shapes=[pltpu.VMEM((parts, rows, width // parts), BF16), dma((parts,))],
        compiler_params=pltpu.CompilerParams(vmem_limit_bytes=LIMIT2),
        name="scale_rows",
    )(attended, scale, rms_gain.reshape(1, width))


def solution(mesh):
    split = P(("groups", "ctx", "head"), None)
    return jax.shard_map(
        functools.partial(per_device, mesh.shape["ctx"], mesh.shape["head"]),
        mesh=mesh,
        in_specs=(split, split, split, P("groups"), P()),
        out_specs=split,
        check_vma=False,
    )
```

```python
import functools

import jax
import jax.numpy as jnp
from jax import lax
from jax.experimental import pallas as pl
from jax.experimental.pallas import tpu as pltpu
from jax.sharding import PartitionSpec as P

DH = 128
MESH = pl.DeviceIdType.MESH
LIMIT1 = 52 << 20
LIMIT2 = 8 << 20
F32 = jnp.float32
BF16 = jnp.bfloat16
BATCH = 4
SKIP = 0
LATE = 4


def silu(v):
    v = v.astype(F32)
    half = 0.5 * v
    return (half + half * jnp.tanh(half)).astype(BF16)


def kernel(nz, nh, group, docs_hbm, q_hbm, k_hbm, v_hbm, out_ref, scale_ref,
           ends_ref, doc_sem, qb, kb, vb, wq, maskb, joinb, keepb, tsend, tt, xout, tin, partial, zin, zout, prefix, pin, st, fin, early,
           load_sem, s_send, s_recv, t_send, t_recv, z_send, z_recv, p_send, p_recv, f_send, f_recv, e_send, e_recv, d_send):
    nx = nh // 2
    rows, width = q_hbm.shape
    heads = width // DH
    half = heads // 2
    own = half // nx
    docs = ends_ref.shape[0]
    chunk = 2 * rows
    shard = nx * chunk
    longest = nz * shard // nh
    chained = longest > shard
    skip = SKIP if nx == 2 and not chained else 0
    z = lax.axis_index("ctx")
    h = lax.axis_index("head")
    x = h // 2
    c = h % 2
    o = 1 - c

    def device(xx, cc, zz=None):
        return {"ctx": z if zz is None else zz, "head": 2 * xx + cc}

    ahead = [lax.rem(x + 1 + s, nx) for s in range(nx)]
    behind = [lax.rem(x + 2 * nx - 1 - s, nx) for s in range(nx)]

    def cols(head, count=1):
        return pl.ds(pl.multiple_of(head * DH, DH), count * DH)

    def first_head(side, s, g):
        return (o if side else c) * half + ahead[s] * own + g * group

    groups = own // group

    tails_used = (z < nz - 1) | (x < nx - 1)

    def load(side, s, g, count, sem):
        at = cols(first_head(side, s, g), count)
        for src, dst in ((k_hbm, kb), (v_hbm, vb)):
            pltpu.make_async_copy(src.at[:, at], dst.at[:, at], load_sem.at[sem]).start()

    def loaded(sem, count):
        at = pl.ds(0, 4 * count * DH)
        pltpu.make_async_copy(k_hbm.at[:, at], kb.at[:, at], load_sem.at[sem]).wait()

    for side in (1, 0):
        load(side, 0, 0, group, 0)
    docs_copy = pltpu.make_async_copy(docs_hbm, ends_ref, doc_sem)
    docs_copy.start()

    barrier = pltpu.get_barrier_semaphore()
    pl.semaphore_signal(barrier, inc=1, device_id=device(x, o), device_id_type=MESH)
    for s in range(nx - 1):
        pl.semaphore_signal(barrier, inc=1, device_id=device(ahead[s], c), device_id_type=MESH)

    if skip:
        @pl.when((x == 0) & (z > 0))
        def _():
            pl.semaphore_signal(barrier, inc=1, device_id=device(1, c, z - 1), device_id_type=MESH)

        @pl.when((x > 0) & (z < nz - 1))
        def _():
            pl.semaphore_signal(barrier, inc=1, device_id=device(0, c, z + 1), device_id_type=MESH)

    across = [ahead[0], behind[0]][:min(nx - 1, 2)]
    for xx in across:
        pl.semaphore_signal(barrier, inc=1, device_id=device(xx, o), device_id_type=MESH)

    @pl.when(z > 0)
    def _():
        pl.semaphore_signal(barrier, inc=1, device_id=device(x, c, z - 1), device_id_type=MESH)

    @pl.when(z < nz - 1)
    def _():
        pl.semaphore_signal(barrier, inc=1, device_id=device(x, c, z + 1), device_id_type=MESH)

    for s in range(nx):
        skip = 0 if s else 1
        if groups > skip:
            for side in (1, 0):
                load(side, s, skip, own - skip * group, s + 1)
    q_copy = pltpu.make_async_copy(q_hbm, qb, load_sem.at[nx + 1])
    q_copy.start()

    def activate(s, g):
        for i in range(group):
            for side in (1, 0):
                at = cols(first_head(side, s, g) + i)
                kb[:, at] = silu(kb[:, at])

    loaded(0, group)
    activate(0, 0)
    docs_copy.wait()
    ends = [ends_ref[0]]
    for d in range(1, docs):
        ends.append(ends[-1] + ends_ref[d])

    def seg_of(pos):
        total = jnp.where(pos < 0, -1, 0)
        for end in ends:
            total = total + jnp.where(pos >= end, 1, 0)
        return total

    def spans(start, count):
        return jnp.where(seg_of(start - 1) == seg_of(start + count - 1), 1.0, 0.0).astype(F32)

    shard_start = z * shard
    chip = shard_start + x * chunk
    first = chip + c * rows
    row_i = lax.broadcasted_iota(jnp.int32, (rows, DH), 0)
    seg_r = seg_of(row_i + first)
    keepb[...] = jnp.where(seg_r == seg_of(first + rows - 1), 1.0, 0.0).astype(BF16)

    def tails(s, g):
        if s == 0 and g == 1:
            loaded(1, own - group)
        elif s and g == 0:
            loaded(s + 1, own)
        for i in range(group):
            for side in (1, 0):
                at = cols(first_head(side, s, g) + i)
                kk = kb[:, at] if s == 0 and g == 0 else silu(kb[:, at])
                kb[:, at] = kk
                t = lax.dot_general(kk * keepb[...], vb[:, at], (((0,), (0,)), ((), ())), preferred_element_type=F32).astype(BF16)
                if side:
                    tsend[s, g * group + i] = t
                else:
                    tt[c, s, g * group + i] = t

    s_copies = {}

    def pass_tails(s, g):
        at = pl.ds(g * group, group)
        cp = pltpu.make_async_remote_copy(
            src_ref=tsend.at[s, at], dst_ref=tt.at[c, s, at], send_sem=s_send, recv_sem=s_recv.at[s, g],
            device_id=device(x, o), device_id_type=MESH)
        cp.start()
        s_copies[s, g] = cp

    t_copies = {}

    def join_tails(s, g):
        s_copies[s, g].wait_recv()
        for i in range(group):
            p = g * group + i
            if s == 0 and p == 0 and nx > 1:
                continue
            t = (tt[1, s, p].astype(F32) + tt[0, s, p].astype(F32) * high).astype(BF16)
            if s == nx - 1:
                tin[s, p] = t
                continue
            xout[s * own + p] = t
            cp = pltpu.make_async_remote_copy(
                src_ref=xout.at[s * own + p], dst_ref=tin.at[s, p], send_sem=t_send, recv_sem=t_recv.at[s, p],
                device_id=device(ahead[s], c), device_id_type=MESH)
            pl.when(tails_used)(cp.start)
            t_copies[s, p] = cp

    tails(0, 0)
    pl.semaphore_wait(barrier, nx + len(across) + jnp.where(z > 0, 2 - x if skip else 1, 0) + jnp.where(z < nz - 1, 1 + x if skip else 1, 0))
    e_copies = []
    if nx > 1:
        for n, (src, cc) in enumerate(((tt.at[c, 0, 0], c), (tsend.at[0, 0], o))):
            cp = pltpu.make_async_remote_copy(
                src_ref=src, dst_ref=early.at[c], send_sem=e_send, recv_sem=e_recv.at[n],
                device_id=device(ahead[0], cc), device_id_type=MESH)
            pl.when(tails_used)(cp.start)
            e_copies.append(cp)
    pass_tails(0, 0)
    joinb[...] = jnp.where(seg_r == seg_of(first - 1), 1.0, 0.0).astype(BF16)
    col_i = lax.broadcasted_iota(jnp.int32, (8, rows), 1)
    seg_c = seg_of(col_i + first)[0:1]
    for g in range(rows // DH):
        sc = jnp.broadcast_to(seg_c[:, g * DH:(g + 1) * DH], (rows, DH))
        ci = lax.broadcasted_iota(jnp.int32, (rows, DH), 1) + g * DH
        maskb[:, g * DH:(g + 1) * DH] = jnp.where((seg_r == sc) & (row_i >= ci), 1.0, 0.0).astype(BF16)
    low = spans(chip, rows)
    high = spans(chip + rows, rows)
    other = spans(shard_start + behind[0] * chunk + rows, rows)
    cont = [spans(shard_start + xx * chunk, chunk) for xx in range(nx)]

    order = [(s, g) for s in range(nx) for g in range(groups)]
    delay = min(3, len(order) - 1)
    for n, (s, g) in enumerate(order):
        if n:
            tails(s, g)
            pass_tails(s, g)
        if n >= delay:
            join_tails(*order[n - delay])
    for s, g in order[len(order) - delay:]:
        join_tails(s, g)

    q_copy.wait()

    def head_of(side, s, p):
        owner = x if s == nx - 1 else behind[s]
        return (o if side else c) * half + owner * own + p

    def local(batch):
        for one in batch:
            head = head_of(*one)
            qq = silu(qb[:, cols(head)])
            scores = lax.dot_general(qq, kb[:, cols(head)], (((1,), (1,)), ((), ())), preferred_element_type=F32)
            wq[head, :, :rows] = scores.astype(BF16) * maskb[...]
            wq[head, :, rows:] = qq * joinb[...]

    @pl.when(z == 0)
    def _():
        zin[...] = jnp.zeros_like(zin)

    @pl.when((z == 0) & (x == 0))
    def _():
        pin[...] = jnp.zeros_like(pin)

    def z_copy(p):
        return pltpu.make_async_remote_copy(
            src_ref=zout.at[p], dst_ref=zin.at[p], send_sem=z_send, recv_sem=z_recv.at[p],
            device_id=device(x, c, z + 1), device_id_type=MESH)

    def receive(p):
        @pl.when(z > 0)
        def _():
            z_copy(p).wait_recv()

    def fold(p):
        for s in range(nx - 1):
            coming = (z < nz - 1) | (behind[s] < nx - 1)
            if s == 0 and p == 0:
                for cp in e_copies:
                    pl.when(coming)(cp.wait_recv)
                tin[0, 0] = (early[1].astype(F32) + early[0].astype(F32) * other).astype(BF16)
                continue
            pl.when(coming)(t_copies[s, p].wait_recv)
        add = None
        for xx in range(nx):
            got = tin[lax.rem(x + 2 * nx - 1 - xx, nx), p].astype(F32)
            add = got if xx == 0 else got + add * cont[xx]
            partial[p, xx] = add
        if chained:
            receive(p)
            whole = 1.0
            for xx in range(nx):
                whole = whole * cont[xx]
            add = add + zin[p].astype(F32) * whole
        zout[p] = add.astype(BF16)

        @pl.when(z < nz - 1)
        def _():
            z_copy(p).start()

        if p >= own - skip * (nz - 2):
            cp = pltpu.make_async_remote_copy(
                src_ref=zout.at[p], dst_ref=pin.at[p], send_sem=d_send.at[own - 1 - p], recv_sem=p_recv.at[0, p],
                device_id=device(0, c, z + 1), device_id_type=MESH)
            cond = (x > 0) & (p >= own - skip * (nz - 2 - z))
            pl.when(cond)(cp.start)
            skips.append((cp, cond))

    skips = []
    p_copies = {}
    f_copies = {}

    def forward(s, p, state):
        into = tt[0, nx - 1 if s == nx - 1 else nx - 2 - s, p].astype(F32) + state.astype(F32) * low
        st[0, s, p] = state
        st[1, s, p] = into.astype(BF16)
        cp = pltpu.make_async_remote_copy(
            src_ref=st.at[o, s, p], dst_ref=fin.at[s, p], send_sem=f_send, recv_sem=f_recv.at[s, p],
            device_id=device(x, o), device_id_type=MESH)
        cp.start()
        f_copies[s, p] = cp

    def spread(p):
        if not chained:
            receive(p)
        carried = zin[p].astype(F32)
        passed = 1.0
        prefix[0, p] = zin[p]
        for xx in range(nx - 1):
            passed = passed * cont[xx]
            prefix[xx + 1, p] = (partial[p, xx] + carried * passed).astype(BF16)
        for s in range(nx - 1):
            cp = pltpu.make_async_remote_copy(
                src_ref=prefix.at[ahead[s], p], dst_ref=pin.at[s * own + p],
                send_sem=p_send, recv_sem=p_recv.at[s, p],
                device_id=device(ahead[s], c), device_id_type=MESH)
            pl.when((ahead[s] > 0) | (z > 0) & (p < own - skip * (nz - 1 - z)) if skip else (ahead[s] > 0) | (z > 0))(cp.start)
            p_copies[s, p] = cp
        forward(nx - 1, p, prefix[x, p])

    def finish(batch, total):
        for side, s, p in batch:
            if side:
                f_copies[s, p].wait_recv()
        for side, s, p in batch:
            head = head_of(side, s, p)
            state = fin[s, p] if side else st[c, s, p]
            both = jnp.concatenate([vb[:, cols(head)], state], axis=0)
            att = jnp.dot(wq[head], both, preferred_element_type=F32).astype(BF16)
            out_ref[:, cols(head)] = att
            att = att.astype(F32)
            total = total + att * att
        return total

    lag = 0 if chained else min(3, own)
    rest = [(s, p) for s in range(nx - 1) for p in range(own)]
    every = [(side, s, p) for s, p in [(nx - 1, p) for p in range(own)] + rest for side in (0, 1)]
    ready = {}
    for n in range(own):
        ready[0, nx - 1, n] = n + lag
        ready[1, nx - 1, n] = n + lag + LATE
    for n, (s, p) in enumerate(rest):
        ready[0, s, p] = n + own
        ready[1, s, p] = n + own + LATE
    slots = own + len(rest)
    waiting = sorted(ready, key=lambda one: (ready[one], one))
    todo = list(every)
    total = jnp.zeros((rows, DH), F32)
    for slot in range(slots):
        if slot < own:
            fold(slot)
        count = -(-len(todo) // max(own - slot, 1))
        local(todo[:count])
        todo = todo[count:]
        if lag <= slot < own + lag:
            spread(slot - lag)
        if slot >= own:
            s, p = rest[slot - own]
            pl.when((z > 0) | (x > 0))(p_copies[s, p].wait_recv)
            forward(s, p, pin[s * own + p])
        now = [one for one in waiting if ready[one] <= slot and one not in todo]
        if len(now) >= BATCH:
            total = finish(now[:BATCH], total)
            waiting = [one for one in waiting if one not in now[:BATCH]]
    while waiting:
        total = finish(waiting[:2], total)
        waiting = waiting[2:]
    scale = lax.rsqrt(jnp.sum(total, axis=1, keepdims=True) / width + 1e-05)
    scale_ref[...] = jnp.broadcast_to(scale, (rows, DH))

    def sent(src, dst, sem, recv):
        pltpu.make_async_remote_copy(
            src_ref=src, dst_ref=dst, send_sem=sem, recv_sem=recv,
            device_id=device(x, o), device_id_type=MESH).wait_send()

    sent(tsend, tt.at[c], s_send, s_recv.at[0, 0])
    if nx > 1:
        @pl.when(tails_used)
        def _():
            late = pl.ds(1, (nx - 1) * own - 1)
            sent(early, early, e_send, e_recv.at[0])
            sent(xout.at[late], xout.at[late], t_send, t_recv.at[0, 0])

    def sent_prefixes(cond, count):
        if count > 0:
            @pl.when(cond)
            def _():
                part = pl.ds(0, count)
                sent(pin.at[part], pin.at[part], p_send, p_recv.at[0, 0])

    if skip:
        sent_prefixes(x == 0, own)
        for zz in range(1, nz):
            sent_prefixes((x > 0) & (z == zz), own - skip * (nz - 1 - zz))
        for cp, cond in skips:
            pl.when(cond)(cp.wait_send)
    else:
        sent_prefixes((z > 0) | (x == 0), (nx - 1) * own)
        sent_prefixes((z == 0) & (x > 0), (nx - 2) * own)
    sent(st.at[o], fin, f_send, f_recv.at[0, 0])

    @pl.when(z < nz - 1)
    def _():
        sent(zout, zin, z_send, z_recv.at[0])


def scale_kernel(parts, att_ref, scale_ref, gain_ref, out_hbm, buf, sem):
    rows, width = att_ref.shape
    part = rows // parts
    for j in range(parts):
        at = pl.ds(j * part, part)
        scale = scale_ref[at, :]
        for i in range(width // DH):
            col = pl.ds(i * DH, DH)
            v = att_ref[at, col].astype(F32)
            buf[at, col] = (v * scale * gain_ref[0:1, col]).astype(BF16)
        pltpu.make_async_copy(buf.at[at], out_hbm.at[at], sem).start()
    pltpu.make_async_copy(buf, out_hbm, sem).wait()


def per_device(nz, nh, queries, keys_in, values, doc_lengths, rms_gain):
    rows, width = queries.shape
    nx = nh // 2
    heads = width // DH
    own = heads // 2 // nx
    group = 2 if own % 2 == 0 else 1
    groups = own // group
    far = max(nx - 1, 1)
    docs = doc_lengths.shape
    vmem = pltpu.VMEM
    full = vmem((rows, width), BF16)
    dma = pltpu.SemaphoreType.DMA
    hbm_spec = pl.BlockSpec(memory_space=pltpu.HBM)
    vmem_spec = pl.BlockSpec(memory_space=pltpu.VMEM)
    attended, scale = pl.pallas_call(
        functools.partial(kernel, nz, nh, group),
        out_shape=(jax.ShapeDtypeStruct((rows, width), BF16), jax.ShapeDtypeStruct((rows, DH), F32)),
        in_specs=[hbm_spec] * 4,
        out_specs=(vmem_spec, vmem_spec),
        scratch_shapes=[
            pltpu.SMEM(docs, jnp.int32), dma(()),
            full, full, full,
            vmem((heads, rows, rows + DH), BF16),
            vmem((rows, rows), BF16),
            vmem((rows, DH), BF16),
            vmem((rows, DH), BF16),
            vmem((nx, own, DH, DH), BF16),
            vmem((2, nx, own, DH, DH), BF16),
            vmem((far * own, DH, DH), BF16),
            vmem((nx, own, DH, DH), BF16),
            vmem((own, nx, DH, DH), F32),
            vmem((own, DH, DH), BF16),
            vmem((own, DH, DH), BF16),
            vmem((nx, own, DH, DH), BF16),
            vmem((far * own, DH, DH), BF16),
            vmem((2, nx, own, DH, DH), BF16),
            vmem((nx, own, DH, DH), BF16),
            vmem((2, DH, DH), BF16),
            dma((nx + 2,)),
            dma(()), dma((nx, groups)),
            dma(()), dma((far, own)),
            dma(()), dma((own,)),
            dma(()), dma((far, own)),
            dma(()), dma((nx, own)),
            dma(()), dma((2,)), dma((max(1, SKIP * (nz - 2)) if nx == 2 else 1,)),
        ],
        compiler_params=pltpu.CompilerParams(collective_id=0, has_side_effects=True, vmem_limit_bytes=LIMIT1),
        name="scan_attention",
    )(pltpu.with_memory_space_constraint(doc_lengths, pltpu.HBM), queries, keys_in, values)
    parts = 8
    return pl.pallas_call(
        functools.partial(scale_kernel, parts),
        out_shape=jax.ShapeDtypeStruct((rows, width), BF16),
        in_specs=[pl.BlockSpec(memory_space=pltpu.VMEM)] * 3,
        out_specs=pl.BlockSpec(memory_space=pl.ANY),
        scratch_shapes=[pltpu.VMEM((rows, width), BF16), dma(())],
        compiler_params=pltpu.CompilerParams(vmem_limit_bytes=LIMIT2),
        name="scale_rows",
    )(attended, scale, rms_gain.reshape(1, width))


def solution(mesh):
    split = P(("groups", "ctx", "head"), None)
    return jax.shard_map(
        functools.partial(per_device, mesh.shape["ctx"], mesh.shape["head"]),
        mesh=mesh,
        in_specs=(split, split, split, P("groups"), P()),
        out_specs=split,
        check_vma=False,
    )
```

```python
import functools

import jax
import jax.numpy as jnp
from jax import lax
from jax.experimental import pallas as pl
from jax.experimental.pallas import tpu as pltpu
from jax.sharding import PartitionSpec as P

DH = 128
MESH = pl.DeviceIdType.MESH
LIMIT1 = 52 << 20
LIMIT2 = 8 << 20
F32 = jnp.float32
BF16 = jnp.bfloat16
BATCH = 4
LATE = 4


def silu(v):
    v = v.astype(F32)
    half = 0.5 * v
    return (half + half * jnp.tanh(half)).astype(BF16)


def kernel(nz, nh, group, docs_hbm, q_hbm, k_hbm, v_hbm, out_ref, scale_ref,
           ends_ref, doc_sem, qb, kb, vb, wq, maskb, joinb, keepb, tsend, tt, xout, tin, partial, zin, zout, prefix, pin, st, fin, early, direct,
           load_sem, s_send, s_recv, t_send, t_recv, z_send, z_recv, p_send, p_recv, f_send, f_recv, e_send, e_recv, d_send, d_recv):
    nx = nh // 2
    rows, width = q_hbm.shape
    heads = width // DH
    half = heads // 2
    own = half // nx
    docs = ends_ref.shape[0]
    chunk = 2 * rows
    shard = nx * chunk
    longest = nz * shard // nh
    chained = longest > shard
    z = lax.axis_index("ctx")
    h = lax.axis_index("head")
    x = h // 2
    c = h % 2
    o = 1 - c

    def device(xx, cc, zz=None):
        return {"ctx": z if zz is None else zz, "head": 2 * xx + cc}

    ahead = [lax.rem(x + 1 + s, nx) for s in range(nx)]
    behind = [lax.rem(x + 2 * nx - 1 - s, nx) for s in range(nx)]

    def cols(head, count=1):
        return pl.ds(pl.multiple_of(head * DH, DH), count * DH)

    def first_head(side, s, g):
        return (o if side else c) * half + ahead[s] * own + g * group

    groups = own // group

    tails_used = (z < nz - 1) | (x < nx - 1)

    def load(side, s, g, count, sem):
        at = cols(first_head(side, s, g), count)
        for src, dst in ((k_hbm, kb), (v_hbm, vb)):
            pltpu.make_async_copy(src.at[:, at], dst.at[:, at], load_sem.at[sem]).start()

    def loaded(sem, count):
        at = pl.ds(0, 4 * count * DH)
        pltpu.make_async_copy(k_hbm.at[:, at], kb.at[:, at], load_sem.at[sem]).wait()

    for side in (1, 0):
        load(side, 0, 0, group, 0)
    docs_copy = pltpu.make_async_copy(docs_hbm, ends_ref, doc_sem)
    docs_copy.start()

    barrier = pltpu.get_barrier_semaphore()
    pl.semaphore_signal(barrier, inc=1, device_id=device(x, o), device_id_type=MESH)
    for s in range(nx - 1):
        pl.semaphore_signal(barrier, inc=1, device_id=device(ahead[s], c), device_id_type=MESH)

    across = [ahead[0], behind[0]][:min(nx - 1, 2)]
    for xx in across:
        pl.semaphore_signal(barrier, inc=1, device_id=device(xx, o), device_id_type=MESH)

    @pl.when(z > 0)
    def _():
        pl.semaphore_signal(barrier, inc=1, device_id=device(x, c, z - 1), device_id_type=MESH)

    @pl.when(z < nz - 1)
    def _():
        pl.semaphore_signal(barrier, inc=1, device_id=device(x, c, z + 1), device_id_type=MESH)

    for s in range(nx):
        skip = 0 if s else 1
        if groups > skip:
            for side in (1, 0):
                load(side, s, skip, own - skip * group, s + 1)
    q_copy = pltpu.make_async_copy(q_hbm, qb, load_sem.at[nx + 1])
    q_copy.start()

    def activate(i):
        for side in (1, 0):
            at = cols(first_head(side, 0, 0) + i)
            kb[:, at] = silu(kb[:, at])

    loaded(0, group)
    activate(0)
    docs_copy.wait()
    ends = [ends_ref[0]]
    for d in range(1, docs):
        ends.append(ends[-1] + ends_ref[d])

    def seg_of(pos):
        total = jnp.where(pos < 0, -1, 0)
        for end in ends:
            total = total + jnp.where(pos >= end, 1, 0)
        return total

    def spans(start, count):
        return jnp.where(seg_of(start - 1) == seg_of(start + count - 1), 1.0, 0.0).astype(F32)

    shard_start = z * shard
    chip = shard_start + x * chunk
    first = chip + c * rows
    row_i = lax.broadcasted_iota(jnp.int32, (rows, DH), 0)
    seg_r = seg_of(row_i + first)
    keepb[...] = jnp.where(seg_r == seg_of(first + rows - 1), 1.0, 0.0).astype(BF16)

    def tails(s, g, begin=0, end=None):
        if s == 0 and g == 1:
            loaded(1, own - group)
        elif s and g == 0:
            loaded(s + 1, own)
        for i in range(begin, group if end is None else end):
            for side in (1, 0):
                at = cols(first_head(side, s, g) + i)
                kk = kb[:, at] if s == 0 and g == 0 and i == 0 else silu(kb[:, at])
                kb[:, at] = kk
                t = lax.dot_general(kk * keepb[...], vb[:, at], (((0,), (0,)), ((), ())), preferred_element_type=F32).astype(BF16)
                if side:
                    tsend[s, g * group + i] = t
                else:
                    tt[c, s, g * group + i] = t

    s_copies = {}

    def pass_tails(s, g):
        at = pl.ds(g * group, group)
        cp = pltpu.make_async_remote_copy(
            src_ref=tsend.at[s, at], dst_ref=tt.at[c, s, at], send_sem=s_send, recv_sem=s_recv.at[s, g],
            device_id=device(x, o), device_id_type=MESH)
        cp.start()
        s_copies[s, g] = cp

    t_copies = {}

    def join_tails(s, g):
        s_copies[s, g].wait_recv()
        for i in range(group):
            p = g * group + i
            if s == 0 and p == 0 and nx > 1:
                continue
            t = (tt[1, s, p].astype(F32) + tt[0, s, p].astype(F32) * high).astype(BF16)
            if s == nx - 1:
                tin[s, p] = t
                continue
            xout[s * own + p] = t
            cp = pltpu.make_async_remote_copy(
                src_ref=xout.at[s * own + p], dst_ref=tin.at[s, p], send_sem=t_send, recv_sem=t_recv.at[s, p],
                device_id=device(ahead[s], c), device_id_type=MESH)
            pl.when(tails_used)(cp.start)
            t_copies[s, p] = cp

    tails(0, 0, 0, 1)
    pl.semaphore_wait(barrier, nx + len(across) + jnp.where(z > 0, 1, 0) + jnp.where(z < nz - 1, 1, 0))
    e_copies = []
    if nx > 1:
        for n, (src, cc) in enumerate(((tt.at[c, 0, 0], c), (tsend.at[0, 0], o))):
            cp = pltpu.make_async_remote_copy(
                src_ref=src, dst_ref=early.at[c], send_sem=e_send, recv_sem=e_recv.at[n],
                device_id=device(ahead[0], cc), device_id_type=MESH)
            pl.when(tails_used)(cp.start)
            e_copies.append(cp)
    tails(0, 0, 1)
    pass_tails(0, 0)
    joinb[...] = jnp.where(seg_r == seg_of(first - 1), 1.0, 0.0).astype(BF16)
    col_i = lax.broadcasted_iota(jnp.int32, (8, rows), 1)
    seg_c = seg_of(col_i + first)[0:1]
    for g in range(rows // DH):
        sc = jnp.broadcast_to(seg_c[:, g * DH:(g + 1) * DH], (rows, DH))
        ci = lax.broadcasted_iota(jnp.int32, (rows, DH), 1) + g * DH
        maskb[:, g * DH:(g + 1) * DH] = jnp.where((seg_r == sc) & (row_i >= ci), 1.0, 0.0).astype(BF16)
    low = spans(chip, rows)
    high = spans(chip + rows, rows)
    other = spans(shard_start + behind[0] * chunk + rows, rows)
    cont = [spans(shard_start + xx * chunk, chunk) for xx in range(nx)]

    order = [(s, g) for s in range(nx) for g in range(groups)]
    delay = min(3, len(order) - 1)
    for n, (s, g) in enumerate(order):
        if n:
            tails(s, g)
            pass_tails(s, g)
        if n >= delay:
            join_tails(*order[n - delay])
    for s, g in order[len(order) - delay:]:
        join_tails(s, g)

    last = (nx - 2, own - 1) if nx > 1 else None
    if nx > 1:
        base_copy = pltpu.make_async_remote_copy(
            src_ref=tt.at[0, 0, own - 1], dst_ref=direct.at[0], send_sem=d_send.at[0], recv_sem=d_recv.at[0],
            device_id=device(x, 1), device_id_type=MESH)
        pl.when(c == 0)(base_copy.start)
        direct_copy = pltpu.make_async_remote_copy(
            src_ref=prefix.at[ahead[nx - 2], own - 1], dst_ref=direct.at[1], send_sem=d_send.at[1], recv_sem=d_recv.at[1],
            device_id=device(ahead[nx - 2], 1), device_id_type=MESH)

    q_copy.wait()

    def head_of(side, s, p):
        owner = x if s == nx - 1 else behind[s]
        return (o if side else c) * half + owner * own + p

    def local(batch):
        for one in batch:
            head = head_of(*one)
            qq = silu(qb[:, cols(head)])
            scores = lax.dot_general(qq, kb[:, cols(head)], (((1,), (1,)), ((), ())), preferred_element_type=F32)
            wq[head, :, :rows] = scores.astype(BF16) * maskb[...]
            wq[head, :, rows:] = qq * joinb[...]

    @pl.when(z == 0)
    def _():
        zin[...] = jnp.zeros_like(zin)

    @pl.when((z == 0) & (x == 0))
    def _():
        pin[...] = jnp.zeros_like(pin)
        direct[1] = jnp.zeros_like(direct[1])

    def z_copy(p):
        return pltpu.make_async_remote_copy(
            src_ref=zout.at[p], dst_ref=zin.at[p], send_sem=z_send, recv_sem=z_recv.at[p],
            device_id=device(x, c, z + 1), device_id_type=MESH)

    def receive(p):
        @pl.when(z > 0)
        def _():
            z_copy(p).wait_recv()

    def fold(p):
        for s in range(nx - 1):
            coming = (z < nz - 1) | (behind[s] < nx - 1)
            if s == 0 and p == 0:
                for cp in e_copies:
                    pl.when(coming)(cp.wait_recv)
                tin[0, 0] = (early[1].astype(F32) + early[0].astype(F32) * other).astype(BF16)
                continue
            pl.when(coming)(t_copies[s, p].wait_recv)
        add = None
        for xx in range(nx):
            got = tin[lax.rem(x + 2 * nx - 1 - xx, nx), p].astype(F32)
            add = got if xx == 0 else got + add * cont[xx]
            partial[p, xx] = add
        if chained:
            receive(p)
            whole = 1.0
            for xx in range(nx):
                whole = whole * cont[xx]
            add = add + zin[p].astype(F32) * whole
        zout[p] = add.astype(BF16)

        @pl.when(z < nz - 1)
        def _():
            z_copy(p).start()

    p_copies = {}
    f_copies = {}

    def forward(s, p, state):
        into = tt[0, nx - 1 if s == nx - 1 else nx - 2 - s, p].astype(F32) + state.astype(F32) * low
        st[0, s, p] = state
        st[1, s, p] = into.astype(BF16)
        cp = pltpu.make_async_remote_copy(
            src_ref=st.at[o, s, p], dst_ref=fin.at[s * own + p], send_sem=f_send, recv_sem=f_recv.at[s, p],
            device_id=device(x, o), device_id_type=MESH)
        if (s, p) == last:
            pl.when(c > 0)(cp.start)
        else:
            cp.start()
        f_copies[s, p] = cp

    def spread(p):
        if not chained:
            receive(p)
        carried = zin[p].astype(F32)
        passed = 1.0
        prefix[0, p] = zin[p]
        for xx in range(nx - 1):
            passed = passed * cont[xx]
            prefix[xx + 1, p] = (partial[p, xx] + carried * passed).astype(BF16)
        for s in range(nx - 1):
            if (s, p) == last:
                pl.when((c == 0) & ((z > 0) | (ahead[s] > 0)))(direct_copy.start)
            cp = pltpu.make_async_remote_copy(
                src_ref=prefix.at[ahead[s], p], dst_ref=pin.at[s * own + p],
                send_sem=p_send, recv_sem=p_recv.at[s, p],
                device_id=device(ahead[s], c), device_id_type=MESH)
            pl.when((z > 0) | (ahead[s] > 0))(cp.start)
            p_copies[s, p] = cp
        forward(nx - 1, p, prefix[x, p])

    def finish(batch, total):
        for side, s, p in batch:
            if side and (s, p) == last:
                pl.when(c == 0)(f_copies[s, p].wait_recv)

                @pl.when(c > 0)
                def _():
                    base_copy.wait_recv()
                    pl.when((z > 0) | (x > 0))(direct_copy.wait_recv)
                    fin[s * own + p] = (direct[0].astype(F32) + direct[1].astype(F32) * low).astype(BF16)
            elif side:
                f_copies[s, p].wait_recv()
        for side, s, p in batch:
            head = head_of(side, s, p)
            state = fin[s * own + p] if side else st[c, s, p]
            both = jnp.concatenate([vb[:, cols(head)], state], axis=0)
            att = jnp.dot(wq[head], both, preferred_element_type=F32).astype(BF16)
            out_ref[:, cols(head)] = att
            att = att.astype(F32)
            total = total + att * att
        return total

    lag = 0 if chained else min(3, own)
    rest = [(s, p) for s in range(nx - 1) for p in range(own)]
    every = [(side, s, p) for s, p in [(nx - 1, p) for p in range(own)] + rest for side in (0, 1)]
    ready = {}
    for n in range(own):
        ready[0, nx - 1, n] = n + lag
        ready[1, nx - 1, n] = n + lag + LATE
    for n, (s, p) in enumerate(rest):
        ready[0, s, p] = n + own
        ready[1, s, p] = n + own + LATE
    slots = own + len(rest)
    waiting = sorted(ready, key=lambda one: (ready[one], one))
    todo = list(every)
    total = jnp.zeros((rows, DH), F32)
    for slot in range(slots):
        if slot < own:
            fold(slot)
        count = -(-len(todo) // max(own - slot, 1))
        local(todo[:count])
        todo = todo[count:]
        if lag <= slot < own + lag:
            spread(slot - lag)
        if slot >= own:
            s, p = rest[slot - own]
            pl.when((z > 0) | (x > 0))(p_copies[s, p].wait_recv)
            forward(s, p, pin[s * own + p])
        now = [one for one in waiting if ready[one] <= slot and one not in todo]
        if len(now) >= BATCH:
            total = finish(now[:BATCH], total)
            waiting = [one for one in waiting if one not in now[:BATCH]]
    while waiting:
        total = finish(waiting[:2], total)
        waiting = waiting[2:]
    scale = lax.rsqrt(jnp.sum(total, axis=1, keepdims=True) / width + 1e-05)
    scale_ref[...] = jnp.broadcast_to(scale, (rows, DH))

    def sent(src, dst, sem, recv):
        pltpu.make_async_remote_copy(
            src_ref=src, dst_ref=dst, send_sem=sem, recv_sem=recv,
            device_id=device(x, o), device_id_type=MESH).wait_send()

    sent(tsend, tt.at[c], s_send, s_recv.at[0, 0])
    if nx > 1:
        @pl.when(tails_used)
        def _():
            late = pl.ds(1, (nx - 1) * own - 1)
            sent(early, early, e_send, e_recv.at[0])
            sent(xout.at[late], xout.at[late], t_send, t_recv.at[0, 0])

    def sent_prefixes(cond, count):
        if count > 0:
            @pl.when(cond)
            def _():
                part = pl.ds(0, count)
                sent(pin.at[part], pin.at[part], p_send, p_recv.at[0, 0])

    sent_prefixes((z > 0) | (x == 0), (nx - 1) * own)
    sent_prefixes((z == 0) & (x > 0), (nx - 2) * own)
    def sent_states(cond, count):
        @pl.when(cond)
        def _():
            part = pl.ds(0, count)
            sent(fin.at[part], fin.at[part], f_send, f_recv.at[0, 0])

    sent_states(c == 0, nx * own - (1 if nx > 1 else 0))
    sent_states(c > 0, nx * own)
    if nx > 1:
        @pl.when(c == 0)
        def _():
            base_copy.wait_send()

        pl.when((c == 0) & ((z > 0) | (ahead[nx - 2] > 0)))(direct_copy.wait_send)

    @pl.when(z < nz - 1)
    def _():
        sent(zout, zin, z_send, z_recv.at[0])


def scale_kernel(parts, att_ref, scale_ref, gain_ref, out_hbm, buf, sem):
    rows, width = att_ref.shape
    part = rows // parts
    for j in range(parts):
        at = pl.ds(j * part, part)
        scale = scale_ref[at, :]
        for i in range(width // DH):
            col = pl.ds(i * DH, DH)
            v = att_ref[at, col].astype(F32)
            buf[at, col] = (v * scale * gain_ref[0:1, col]).astype(BF16)
        pltpu.make_async_copy(buf.at[at], out_hbm.at[at], sem).start()
    pltpu.make_async_copy(buf, out_hbm, sem).wait()


def per_device(nz, nh, queries, keys_in, values, doc_lengths, rms_gain):
    rows, width = queries.shape
    nx = nh // 2
    heads = width // DH
    own = heads // 2 // nx
    group = 2 if own % 2 == 0 else 1
    groups = own // group
    far = max(nx - 1, 1)
    docs = doc_lengths.shape
    vmem = pltpu.VMEM
    full = vmem((rows, width), BF16)
    dma = pltpu.SemaphoreType.DMA
    hbm_spec = pl.BlockSpec(memory_space=pltpu.HBM)
    vmem_spec = pl.BlockSpec(memory_space=pltpu.VMEM)
    attended, scale = pl.pallas_call(
        functools.partial(kernel, nz, nh, group),
        out_shape=(jax.ShapeDtypeStruct((rows, width), BF16), jax.ShapeDtypeStruct((rows, DH), F32)),
        in_specs=[hbm_spec] * 4,
        out_specs=(vmem_spec, vmem_spec),
        scratch_shapes=[
            pltpu.SMEM(docs, jnp.int32), dma(()),
            full, full, full,
            vmem((heads, rows, rows + DH), BF16),
            vmem((rows, rows), BF16),
            vmem((rows, DH), BF16),
            vmem((rows, DH), BF16),
            vmem((nx, own, DH, DH), BF16),
            vmem((2, nx, own, DH, DH), BF16),
            vmem((far * own, DH, DH), BF16),
            vmem((nx, own, DH, DH), BF16),
            vmem((own, nx, DH, DH), F32),
            vmem((own, DH, DH), BF16),
            vmem((own, DH, DH), BF16),
            vmem((nx, own, DH, DH), BF16),
            vmem((far * own, DH, DH), BF16),
            vmem((2, nx, own, DH, DH), BF16),
            vmem((nx * own, DH, DH), BF16),
            vmem((2, DH, DH), BF16),
            vmem((2, DH, DH), BF16),
            dma((nx + 2,)),
            dma(()), dma((nx, groups)),
            dma(()), dma((far, own)),
            dma(()), dma((own,)),
            dma(()), dma((far, own)),
            dma(()), dma((nx, own)),
            dma(()), dma((2,)),
            dma((2,)), dma((2,)),
        ],
        compiler_params=pltpu.CompilerParams(collective_id=0, has_side_effects=True, vmem_limit_bytes=LIMIT1),
        name="scan_attention",
    )(pltpu.with_memory_space_constraint(doc_lengths, pltpu.HBM), queries, keys_in, values)
    parts = 8
    return pl.pallas_call(
        functools.partial(scale_kernel, parts),
        out_shape=jax.ShapeDtypeStruct((rows, width), BF16),
        in_specs=[pl.BlockSpec(memory_space=pltpu.VMEM)] * 3,
        out_specs=pl.BlockSpec(memory_space=pl.ANY),
        scratch_shapes=[pltpu.VMEM((rows, width), BF16), dma(())],
        compiler_params=pltpu.CompilerParams(vmem_limit_bytes=LIMIT2),
        name="scale_rows",
    )(attended, scale, rms_gain.reshape(1, width))


def solution(mesh):
    split = P(("groups", "ctx", "head"), None)
    return jax.shard_map(
        functools.partial(per_device, mesh.shape["ctx"], mesh.shape["head"]),
        mesh=mesh,
        in_specs=(split, split, split, P("groups"), P()),
        out_specs=split,
        check_vma=False,
    )
```

```python
import functools

import jax
import jax.numpy as jnp
from jax import lax
from jax.experimental import pallas as pl
from jax.experimental.pallas import tpu as pltpu
from jax.sharding import PartitionSpec as P

DH = 128
MESH = pl.DeviceIdType.MESH
LIMIT1 = 52 << 20
LIMIT2 = 8 << 20
F32 = jnp.float32
BF16 = jnp.bfloat16
BATCH = 4
LATE = 3


def silu(v):
    v = v.astype(F32)
    half = 0.5 * v
    return (half + half * jnp.tanh(half)).astype(BF16)


def kernel(nz, nh, group, docs_hbm, q_hbm, k_hbm, v_hbm, out_ref, scale_ref,
           ends_ref, doc_sem, qb, kb, vb, wq, maskb, joinb, keepb, tsend, tt, xout, tin, partial, zin, zout, prefix, pin, st, fin, early, direct, sums,
           load_sem, s_send, s_recv, t_send, t_recv, z_send, z_recv, p_send, p_recv, f_recv, e_recv, d_recv):
    nx = nh // 2
    rows, width = q_hbm.shape
    heads = width // DH
    half = heads // 2
    own = half // nx
    docs = ends_ref.shape[0]
    chunk = 2 * rows
    shard = nx * chunk
    longest = nz * shard // nh
    chained = longest > shard
    z = lax.axis_index("ctx")
    h = lax.axis_index("head")
    x = h // 2
    c = h % 2
    o = 1 - c

    def device(xx, cc, zz=None):
        return {"ctx": z if zz is None else zz, "head": 2 * xx + cc}

    ahead = [lax.rem(x + 1 + s, nx) for s in range(nx)]
    behind = [lax.rem(x + 2 * nx - 1 - s, nx) for s in range(nx)]

    def cols(head, count=1):
        return pl.ds(pl.multiple_of(head * DH, DH), count * DH)

    def first_head(side, s, g):
        return (o if side else c) * half + ahead[s] * own + g * group

    groups = own // group

    tails_used = (z < nz - 1) | (x < nx - 1)

    def load(side, s, g, count, sem):
        at = cols(first_head(side, s, g), count)
        for src, dst in ((k_hbm, kb), (v_hbm, vb)):
            pltpu.make_async_copy(src.at[:, at], dst.at[:, at], load_sem.at[sem]).start()

    def loaded(sem, count):
        at = pl.ds(0, 4 * count * DH)
        pltpu.make_async_copy(k_hbm.at[:, at], kb.at[:, at], load_sem.at[sem]).wait()

    for side in (1, 0):
        load(side, 0, 0, group, 0)
    docs_copy = pltpu.make_async_copy(docs_hbm, ends_ref, doc_sem)
    docs_copy.start()

    barrier = pltpu.get_barrier_semaphore()
    pl.semaphore_signal(barrier, inc=1, device_id=device(x, o), device_id_type=MESH)
    for s in range(nx - 1):
        pl.semaphore_signal(barrier, inc=1, device_id=device(ahead[s], c), device_id_type=MESH)

    across = [ahead[0], behind[0]][:min(nx - 1, 2)]
    for xx in across:
        pl.semaphore_signal(barrier, inc=1, device_id=device(xx, o), device_id_type=MESH)

    @pl.when(z > 0)
    def _():
        pl.semaphore_signal(barrier, inc=1, device_id=device(x, c, z - 1), device_id_type=MESH)

    @pl.when(z < nz - 1)
    def _():
        pl.semaphore_signal(barrier, inc=1, device_id=device(x, c, z + 1), device_id_type=MESH)

    for s in range(nx):
        skip = 0 if s else 1
        if groups > skip:
            for side in (1, 0):
                load(side, s, skip, own - skip * group, s + 1)
    q_copy = pltpu.make_async_copy(q_hbm, qb, load_sem.at[nx + 1])
    q_copy.start()

    def activate(i):
        for side in (1, 0):
            at = cols(first_head(side, 0, 0) + i)
            kb[:, at] = silu(kb[:, at])

    loaded(0, group)
    activate(0)
    docs_copy.wait()
    ends = [ends_ref[0]]
    for d in range(1, docs):
        ends.append(ends[-1] + ends_ref[d])

    def seg_of(pos):
        total = jnp.where(pos < 0, -1, 0)
        for end in ends:
            total = total + jnp.where(pos >= end, 1, 0)
        return total

    def spans(start, count):
        return jnp.where(seg_of(start - 1) == seg_of(start + count - 1), 1.0, 0.0).astype(F32)

    shard_start = z * shard
    chip = shard_start + x * chunk
    first = chip + c * rows
    row_i = lax.broadcasted_iota(jnp.int32, (rows, DH), 0)
    seg_r = seg_of(row_i + first)
    keepb[...] = jnp.where(seg_r == seg_of(first + rows - 1), 1.0, 0.0).astype(BF16)

    def tails(s, g, begin=0, end=None):
        if s == 0 and g == 1:
            loaded(1, own - group)
        elif s and g == 0:
            loaded(s + 1, own)
        for i in range(begin, group if end is None else end):
            for side in (1, 0):
                at = cols(first_head(side, s, g) + i)
                kk = kb[:, at] if s == 0 and g == 0 and i == 0 else silu(kb[:, at])
                kb[:, at] = kk
                t = lax.dot_general(kk * keepb[...], vb[:, at], (((0,), (0,)), ((), ())), preferred_element_type=F32).astype(BF16)
                if side:
                    tsend[s, g * group + i] = t
                else:
                    tt[c, s, g * group + i] = t

    s_copies = {}
    wide = 2 if groups % 2 == 0 else 1

    def pass_tails(s, g):
        count = wide if s else 1
        at = pl.ds((g + 1 - count) * group, count * group)
        cp = pltpu.make_async_remote_copy(
            src_ref=tsend.at[s, at], dst_ref=tt.at[c, s, at], send_sem=s_send, recv_sem=s_recv.at[s, g],
            device_id=device(x, o), device_id_type=MESH)
        cp.start()
        s_copies[s, g] = cp

    t_copies = {}

    def join_tails(s, g):
        if s == 0 or g % wide == 0:
            s_copies[s, g if s == 0 else g + wide - 1].wait_recv()
        for i in range(group):
            p = g * group + i
            if s == 0 and p == 0 and nx > 1:
                continue
            t = (tt[1, s, p].astype(F32) + tt[0, s, p].astype(F32) * high).astype(BF16)
            if s == nx - 1:
                tin[s, p] = t
                continue
            xout[s * own + p] = t
            cp = pltpu.make_async_remote_copy(
                src_ref=xout.at[s * own + p], dst_ref=tin.at[s, p], send_sem=t_send, recv_sem=t_recv.at[s, p],
                device_id=device(ahead[s], c), device_id_type=MESH)
            pl.when(tails_used)(cp.start)
            t_copies[s, p] = cp

    tails(0, 0, 0, 1)
    pl.semaphore_wait(barrier, nx + len(across) + jnp.where(z > 0, 1, 0) + jnp.where(z < nz - 1, 1, 0))
    e_copies = []
    if nx > 1:
        for n, (src, cc) in enumerate(((tt.at[c, 0, 0], c), (tsend.at[0, 0], o))):
            cp = pltpu.make_async_remote_copy(
                src_ref=src, dst_ref=early.at[c], send_sem=t_send, recv_sem=t_recv.at[0, 0] if n == 0 else e_recv,
                device_id=device(ahead[0], cc), device_id_type=MESH)
            pl.when(tails_used)(cp.start)
            e_copies.append(cp)
    tails(0, 0, 1)
    pass_tails(0, 0)
    joinb[...] = jnp.where(seg_r == seg_of(first - 1), 1.0, 0.0).astype(BF16)
    col_i = lax.broadcasted_iota(jnp.int32, (8, rows), 1)
    seg_c = seg_of(col_i + first)[0:1]
    for g in range(rows // DH):
        sc = jnp.broadcast_to(seg_c[:, g * DH:(g + 1) * DH], (rows, DH))
        ci = lax.broadcasted_iota(jnp.int32, (rows, DH), 1) + g * DH
        maskb[:, g * DH:(g + 1) * DH] = jnp.where((seg_r == sc) & (row_i >= ci), 1.0, 0.0).astype(BF16)
    low = spans(chip, rows)
    high = spans(chip + rows, rows)
    other = spans(shard_start + behind[0] * chunk + rows, rows)
    cont = [spans(shard_start + xx * chunk, chunk) for xx in range(nx)]

    order = [(s, g) for s in range(nx) for g in range(groups)]
    delay = min(3, len(order) - 1)
    for n, (s, g) in enumerate(order):
        if n:
            tails(s, g)
            if s == 0 or g % wide == wide - 1:
                pass_tails(s, g)
        if n >= delay:
            join_tails(*order[n - delay])
    for s, g in order[len(order) - delay:]:
        join_tails(s, g)

    last = (nx - 2, own - 1) if nx > 1 else None
    if nx > 1:
        base_copy = pltpu.make_async_remote_copy(
            src_ref=tt.at[0, 0, own - 1], dst_ref=direct.at[0], send_sem=s_send, recv_sem=d_recv.at[0],
            device_id=device(x, 1), device_id_type=MESH)
        pl.when(c == 0)(base_copy.start)
        direct_copy = pltpu.make_async_remote_copy(
            src_ref=prefix.at[ahead[nx - 2], own - 1], dst_ref=direct.at[1], send_sem=p_send, recv_sem=d_recv.at[1],
            device_id=device(ahead[nx - 2], 1), device_id_type=MESH)

    q_copy.wait()

    def head_of(side, s, p):
        owner = x if s == nx - 1 else behind[s]
        return (o if side else c) * half + owner * own + p

    def local(batch):
        for one in batch:
            head = head_of(*one)
            qq = silu(qb[:, cols(head)])
            scores = lax.dot_general(qq, kb[:, cols(head)], (((1,), (1,)), ((), ())), preferred_element_type=F32)
            wq[head, :, :rows] = scores.astype(BF16) * maskb[...]
            wq[head, :, rows:] = qq * joinb[...]

    @pl.when(z == 0)
    def _():
        zin[...] = jnp.zeros_like(zin)

    @pl.when((z == 0) & (x == 0))
    def _():
        pin[...] = jnp.zeros_like(pin)
        direct[1] = jnp.zeros_like(direct[1])

    def z_copy(p):
        return pltpu.make_async_remote_copy(
            src_ref=zout.at[p], dst_ref=zin.at[p], send_sem=z_send, recv_sem=z_recv.at[p],
            device_id=device(x, c, z + 1), device_id_type=MESH)

    def receive(p):
        @pl.when(z > 0)
        def _():
            z_copy(p).wait_recv()

    def fold(p):
        for s in range(nx - 1):
            coming = (z < nz - 1) | (behind[s] < nx - 1)
            if s == 0 and p == 0:
                for cp in e_copies:
                    pl.when(coming)(cp.wait_recv)
                tin[0, 0] = (early[1].astype(F32) + early[0].astype(F32) * other).astype(BF16)
                continue
            pl.when(coming)(t_copies[s, p].wait_recv)
        add = None
        for xx in range(nx):
            got = tin[lax.rem(x + 2 * nx - 1 - xx, nx), p].astype(F32)
            add = got if xx == 0 else got + add * cont[xx]
            partial[p, xx] = add
        if chained:
            receive(p)
            whole = 1.0
            for xx in range(nx):
                whole = whole * cont[xx]
            add = add + zin[p].astype(F32) * whole
        zout[p] = add.astype(BF16)

        @pl.when(z < nz - 1)
        def _():
            z_copy(p).start()

    p_copies = {}
    f_copies = {}

    def forward(s, p, state):
        into = tt[0, nx - 1 if s == nx - 1 else nx - 2 - s, p].astype(F32) + state.astype(F32) * low
        st[0, s, p] = state
        st[1, s, p] = into.astype(BF16)
        cp = pltpu.make_async_remote_copy(
            src_ref=st.at[o, s, p], dst_ref=fin.at[s * own + p], send_sem=s_send, recv_sem=f_recv.at[s, p],
            device_id=device(x, o), device_id_type=MESH)
        if (s, p) == last:
            pl.when(c > 0)(cp.start)
        else:
            cp.start()
        f_copies[s, p] = cp

    def spread(p):
        if not chained:
            receive(p)
        carried = zin[p].astype(F32)
        passed = 1.0
        prefix[0, p] = zin[p]
        for xx in range(nx - 1):
            passed = passed * cont[xx]
            prefix[xx + 1, p] = (partial[p, xx] + carried * passed).astype(BF16)
        for s in range(nx - 1):
            if (s, p) == last:
                pl.when((c == 0) & ((z > 0) | (ahead[s] > 0)))(direct_copy.start)
            cp = pltpu.make_async_remote_copy(
                src_ref=prefix.at[ahead[s], p], dst_ref=pin.at[s * own + p],
                send_sem=p_send, recv_sem=p_recv.at[s, p],
                device_id=device(ahead[s], c), device_id_type=MESH)
            pl.when((z > 0) | (ahead[s] > 0))(cp.start)
            p_copies[s, p] = cp
        forward(nx - 1, p, prefix[x, p])

    def finish(batch, total):
        for side, s, p in batch:
            if side and (s, p) == last:
                pl.when(c == 0)(f_copies[s, p].wait_recv)

                @pl.when(c > 0)
                def _():
                    base_copy.wait_recv()
                    pl.when((z > 0) | (x > 0))(direct_copy.wait_recv)
                    fin[s * own + p] = (direct[0].astype(F32) + direct[1].astype(F32) * low).astype(BF16)
            elif side:
                f_copies[s, p].wait_recv()
        for side, s, p in batch:
            head = head_of(side, s, p)
            state = fin[s * own + p] if side else st[c, s, p]
            both = jnp.concatenate([vb[:, cols(head)], state], axis=0)
            att = jnp.dot(wq[head], both, preferred_element_type=F32).astype(BF16)
            out_ref[:, cols(head)] = att
            att = att.astype(F32)
            total = total + att * att
        return total

    lag = 0 if chained else min(3, own)
    rest = [(s, p) for s in range(nx - 1) for p in range(own)]
    every = [(side, s, p) for s, p in [(nx - 1, p) for p in range(own)] + rest for side in (0, 1)]
    ready = {}
    for n in range(own):
        ready[0, nx - 1, n] = n + lag
        ready[1, nx - 1, n] = n + lag + LATE
    for n, (s, p) in enumerate(rest):
        ready[0, s, p] = n + own
        ready[1, s, p] = n + own + LATE
    slots = own + len(rest)
    waiting = sorted(ready, key=lambda one: (ready[one], one))
    todo = list(every)
    total = jnp.zeros((rows, DH), F32)
    for slot in range(slots):
        if slot < own:
            fold(slot)
        count = -(-len(todo) // max(own - slot, 1))
        local(todo[:count])
        todo = todo[count:]
        if lag <= slot < own + lag:
            spread(slot - lag)
        if slot >= own:
            s, p = rest[slot - own]
            pl.when((z > 0) | (x > 0))(p_copies[s, p].wait_recv)
            forward(s, p, pin[s * own + p])
        now = [one for one in waiting if ready[one] <= slot and one not in todo]
        if len(now) >= (BATCH if slot < own else 2):
            total = finish(now[:BATCH], total)
            waiting = [one for one in waiting if one not in now[:BATCH]]
    sums[...] = total

    @pl.when(c == 0)
    def _():
        sums[...] = finish(waiting, sums[...])

    @pl.when(c > 0)
    def _():
        ends_with = [(1, *one) for one in rest[-1:] + rest[-2:-1]]
        others = [one for one in waiting if one not in ends_with]
        sums[...] = finish(others, sums[...])
        for one in ends_with:
            sums[...] = finish([one], sums[...])

    total = sums[...]
    scale = lax.rsqrt(jnp.sum(total, axis=1, keepdims=True) / width + 1e-05)
    scale_ref[...] = jnp.broadcast_to(scale, (rows, DH))

    def sent(src, dst, sem, recv):
        pltpu.make_async_remote_copy(
            src_ref=src, dst_ref=dst, send_sem=sem, recv_sem=recv,
            device_id=device(x, o), device_id_type=MESH).wait_send()

    def sent_if(cond, count, sem):
        if count > 0:
            @pl.when(cond)
            def _():
                part = pl.ds(0, count)
                sent(fin.at[part], fin.at[part], sem, s_recv.at[0, 0])

    sent(tt, tt, s_send, s_recv.at[0, 0])
    if nx > 1:
        sent_if(tails_used, (nx - 1) * own + 1, t_send)
        whole = (z > 0) | (x == 0)
        straight = (c == 0) & ((z > 0) | (ahead[nx - 2] > 0))
        for cond, count in ((whole, (nx - 1) * own), (~whole, (nx - 2) * own)):
            sent_if(cond & straight, count + 1, p_send)
            sent_if(cond & ~straight, count, p_send)

    @pl.when(z < nz - 1)
    def _():
        sent(zout, zin, z_send, z_recv.at[0])


def scale_kernel(parts, att_ref, scale_ref, gain_ref, out_hbm, buf, sem):
    rows, width = att_ref.shape
    part = rows // parts
    for j in range(parts):
        at = pl.ds(j * part, part)
        scale = scale_ref[at, :]
        for i in range(width // DH):
            col = pl.ds(i * DH, DH)
            v = att_ref[at, col].astype(F32)
            buf[at, col] = (v * scale * gain_ref[0:1, col]).astype(BF16)
        pltpu.make_async_copy(buf.at[at], out_hbm.at[at], sem).start()
    pltpu.make_async_copy(buf, out_hbm, sem).wait()


def per_device(nz, nh, queries, keys_in, values, doc_lengths, rms_gain):
    rows, width = queries.shape
    nx = nh // 2
    heads = width // DH
    own = heads // 2 // nx
    group = 2 if own % 2 == 0 else 1
    groups = own // group
    far = max(nx - 1, 1)
    docs = doc_lengths.shape
    vmem = pltpu.VMEM
    full = vmem((rows, width), BF16)
    dma = pltpu.SemaphoreType.DMA
    hbm_spec = pl.BlockSpec(memory_space=pltpu.HBM)
    vmem_spec = pl.BlockSpec(memory_space=pltpu.VMEM)
    attended, scale = pl.pallas_call(
        functools.partial(kernel, nz, nh, group),
        out_shape=(jax.ShapeDtypeStruct((rows, width), BF16), jax.ShapeDtypeStruct((rows, DH), F32)),
        in_specs=[hbm_spec] * 4,
        out_specs=(vmem_spec, vmem_spec),
        scratch_shapes=[
            pltpu.SMEM(docs, jnp.int32), dma(()),
            full, full, full,
            vmem((heads, rows, rows + DH), BF16),
            vmem((rows, rows), BF16),
            vmem((rows, DH), BF16),
            vmem((rows, DH), BF16),
            vmem((nx, own, DH, DH), BF16),
            vmem((2, nx, own, DH, DH), BF16),
            vmem((far * own, DH, DH), BF16),
            vmem((nx, own, DH, DH), BF16),
            vmem((own, nx, DH, DH), F32),
            vmem((own, DH, DH), BF16),
            vmem((own, DH, DH), BF16),
            vmem((nx, own, DH, DH), BF16),
            vmem((far * own, DH, DH), BF16),
            vmem((2, nx, own, DH, DH), BF16),
            vmem((nx * own, DH, DH), BF16),
            vmem((2, DH, DH), BF16),
            vmem((2, DH, DH), BF16),
            vmem((rows, DH), F32),
            dma((nx + 2,)),
            dma(()), dma((nx, groups)),
            dma(()), dma((far, own)),
            dma(()), dma((own,)),
            dma(()), dma((far, own)),
            dma((nx, own)),
            dma(()),
            dma((2,)),
        ],
        compiler_params=pltpu.CompilerParams(collective_id=0, has_side_effects=True, vmem_limit_bytes=LIMIT1),
        name="scan_attention",
    )(pltpu.with_memory_space_constraint(doc_lengths, pltpu.HBM), queries, keys_in, values)
    parts = 8
    return pl.pallas_call(
        functools.partial(scale_kernel, parts),
        out_shape=jax.ShapeDtypeStruct((rows, width), BF16),
        in_specs=[pl.BlockSpec(memory_space=pltpu.VMEM)] * 3,
        out_specs=pl.BlockSpec(memory_space=pl.ANY),
        scratch_shapes=[pltpu.VMEM((rows, width), BF16), dma(())],
        compiler_params=pltpu.CompilerParams(vmem_limit_bytes=LIMIT2),
        name="scale_rows",
    )(attended, scale, rms_gain.reshape(1, width))


def solution(mesh):
    split = P(("groups", "ctx", "head"), None)
    return jax.shard_map(
        functools.partial(per_device, mesh.shape["ctx"], mesh.shape["head"]),
        mesh=mesh,
        in_specs=(split, split, split, P("groups"), P()),
        out_specs=split,
        check_vma=False,
    )
```

```python
import functools

import jax
import jax.numpy as jnp
from jax import lax
from jax.experimental import pallas as pl
from jax.experimental.pallas import tpu as pltpu
from jax.sharding import PartitionSpec as P

DH = 128
MESH = pl.DeviceIdType.MESH
LIMIT1 = 52 << 20
LIMIT2 = 8 << 20
F32 = jnp.float32
BF16 = jnp.bfloat16
BATCH = 4
LATE = 3


def silu(v):
    v = v.astype(F32)
    half = 0.5 * v
    return (half + half * jnp.tanh(half)).astype(BF16)


def kernel(nz, nh, group, docs_hbm, q_hbm, k_hbm, v_hbm, out_ref, scale_ref,
           ends_ref, doc_sem, qb, kb, vb, wq, maskb, joinb, keepb, tsend, tt, xout, tin, partial, zin, zout, prefix, pin, st, fin, early, direct, sums,
           load_sem, s_send, s_recv, t_send, t_recv, z_send, z_recv, p_send, p_recv, f_recv, e_recv, d_recv):
    nx = nh // 2
    rows, width = q_hbm.shape
    heads = width // DH
    half = heads // 2
    own = half // nx
    docs = ends_ref.shape[0]
    chunk = 2 * rows
    shard = nx * chunk
    longest = nz * shard // nh
    chained = longest > shard
    z = lax.axis_index("ctx")
    h = lax.axis_index("head")
    x = h // 2
    c = h % 2
    o = 1 - c

    def device(xx, cc, zz=None):
        return {"ctx": z if zz is None else zz, "head": 2 * xx + cc}

    ahead = [lax.rem(x + 1 + s, nx) for s in range(nx)]
    behind = [lax.rem(x + 2 * nx - 1 - s, nx) for s in range(nx)]

    def cols(head, count=1):
        return pl.ds(pl.multiple_of(head * DH, DH), count * DH)

    def first_head(side, s, g):
        return (o if side else c) * half + ahead[s] * own + g * group

    groups = own // group

    tails_used = (z < nz - 1) | (x < nx - 1)

    def load(side, s, g, count, sem):
        at = cols(first_head(side, s, g), count)
        for src, dst in ((k_hbm, kb), (v_hbm, vb)):
            pltpu.make_async_copy(src.at[:, at], dst.at[:, at], load_sem.at[sem]).start()

    def loaded(sem, count):
        at = pl.ds(0, 4 * count * DH)
        pltpu.make_async_copy(k_hbm.at[:, at], kb.at[:, at], load_sem.at[sem]).wait()

    for side in (1, 0):
        load(side, 0, 0, group, 0)
    docs_copy = pltpu.make_async_copy(docs_hbm, ends_ref, doc_sem)
    docs_copy.start()

    barrier = pltpu.get_barrier_semaphore()
    pl.semaphore_signal(barrier, inc=1, device_id=device(x, o), device_id_type=MESH)
    for s in range(nx - 1):
        pl.semaphore_signal(barrier, inc=1, device_id=device(ahead[s], c), device_id_type=MESH)

    across = [ahead[0], behind[0]][:min(nx - 1, 2)]
    for xx in across:
        pl.semaphore_signal(barrier, inc=1, device_id=device(xx, o), device_id_type=MESH)

    @pl.when(z > 0)
    def _():
        pl.semaphore_signal(barrier, inc=1, device_id=device(x, c, z - 1), device_id_type=MESH)

    @pl.when(z < nz - 1)
    def _():
        pl.semaphore_signal(barrier, inc=1, device_id=device(x, c, z + 1), device_id_type=MESH)

    for s in range(nx):
        skip = 0 if s else 1
        if groups > skip:
            for side in (1, 0):
                load(side, s, skip, own - skip * group, s + 1)
    q_copy = pltpu.make_async_copy(q_hbm, qb, load_sem.at[nx + 1])
    q_copy.start()

    def activate(i):
        for side in (1, 0):
            at = cols(first_head(side, 0, 0) + i)
            kb[:, at] = silu(kb[:, at])

    loaded(0, group)
    activate(0)
    docs_copy.wait()
    ends = [ends_ref[0]]
    for d in range(1, docs):
        ends.append(ends[-1] + ends_ref[d])

    def seg_of(pos):
        total = jnp.where(pos < 0, -1, 0)
        for end in ends:
            total = total + jnp.where(pos >= end, 1, 0)
        return total

    def spans(start, count):
        return jnp.where(seg_of(start - 1) == seg_of(start + count - 1), 1.0, 0.0).astype(F32)

    shard_start = z * shard
    chip = shard_start + x * chunk
    first = chip + c * rows
    row_i = lax.broadcasted_iota(jnp.int32, (rows, DH), 0)
    seg_r = seg_of(row_i + first)
    keepb[...] = jnp.where(seg_r == seg_of(first + rows - 1), 1.0, 0.0).astype(BF16)

    def tails(s, g, begin=0, end=None):
        if s == 0 and g == 1:
            loaded(1, own - group)
        elif s and g == 0:
            loaded(s + 1, own)
        for i in range(begin, group if end is None else end):
            for side in (1, 0):
                at = cols(first_head(side, s, g) + i)
                kk = kb[:, at] if s == 0 and g == 0 and i == 0 else silu(kb[:, at])
                kb[:, at] = kk
                t = lax.dot_general(kk * keepb[...], vb[:, at], (((0,), (0,)), ((), ())), preferred_element_type=F32).astype(BF16)
                if side:
                    tsend[s, g * group + i] = t
                else:
                    tt[c, s, g * group + i] = t

    s_copies = {}
    wide = 2 if groups % 2 == 0 else 1

    def pass_tails(s, g):
        count = wide if s else 1
        at = pl.ds((g + 1 - count) * group, count * group)
        cp = pltpu.make_async_remote_copy(
            src_ref=tsend.at[s, at], dst_ref=tt.at[c, s, at], send_sem=s_send, recv_sem=s_recv.at[g if s == 0 else groups + (s - 1) * (groups // wide) + g // wide],
            device_id=device(x, o), device_id_type=MESH)
        cp.start()
        s_copies[s, g] = cp

    t_copies = {}

    def join_tails(s, g):
        if s == 0 or g % wide == 0:
            s_copies[s, g if s == 0 else g + wide - 1].wait_recv()
        for i in range(group):
            p = g * group + i
            if s == 0 and p == 0 and nx > 1:
                continue
            t = (tt[1, s, p].astype(F32) + tt[0, s, p].astype(F32) * high).astype(BF16)
            if s == nx - 1:
                tin[s, p] = t
                continue
            xout[s * own + p] = t
            cp = pltpu.make_async_remote_copy(
                src_ref=xout.at[s * own + p], dst_ref=tin.at[s, p], send_sem=t_send, recv_sem=t_recv.at[s, p],
                device_id=device(ahead[s], c), device_id_type=MESH)
            pl.when(tails_used)(cp.start)
            t_copies[s, p] = cp

    tails(0, 0, 0, 1)
    pl.semaphore_wait(barrier, nx + len(across) + jnp.where(z > 0, 1, 0) + jnp.where(z < nz - 1, 1, 0))
    e_copies = []
    if nx > 1:
        for n, (src, cc) in enumerate(((tt.at[c, 0, 0], c), (tsend.at[0, 0], o))):
            cp = pltpu.make_async_remote_copy(
                src_ref=src, dst_ref=early.at[c], send_sem=t_send, recv_sem=t_recv.at[0, 0] if n == 0 else e_recv,
                device_id=device(ahead[0], cc), device_id_type=MESH)
            pl.when(tails_used)(cp.start)
            e_copies.append(cp)
    tails(0, 0, 1)
    pass_tails(0, 0)
    joinb[...] = jnp.where(seg_r == seg_of(first - 1), 1.0, 0.0).astype(BF16)
    col_i = lax.broadcasted_iota(jnp.int32, (8, rows), 1)
    seg_c = seg_of(col_i + first)[0:1]
    for g in range(rows // DH):
        sc = jnp.broadcast_to(seg_c[:, g * DH:(g + 1) * DH], (rows, DH))
        ci = lax.broadcasted_iota(jnp.int32, (rows, DH), 1) + g * DH
        maskb[:, g * DH:(g + 1) * DH] = jnp.where((seg_r == sc) & (row_i >= ci), 1.0, 0.0).astype(BF16)
    low = spans(chip, rows)
    high = spans(chip + rows, rows)
    other = spans(shard_start + behind[0] * chunk + rows, rows)
    cont = [spans(shard_start + xx * chunk, chunk) for xx in range(nx)]

    order = [(s, g) for s in range(nx) for g in range(groups)]
    delay = min(4, len(order) - 1)
    for n, (s, g) in enumerate(order):
        if n:
            tails(s, g)
            if s == 0 or g % wide == wide - 1:
                pass_tails(s, g)
        if n >= delay:
            join_tails(*order[n - delay])
    for s, g in order[len(order) - delay:]:
        join_tails(s, g)

    last = (nx - 2, own - 1) if nx > 1 else None
    if nx > 1:
        base_copy = pltpu.make_async_remote_copy(
            src_ref=tt.at[0, 0, own - 1], dst_ref=direct.at[0], send_sem=s_send, recv_sem=d_recv.at[0],
            device_id=device(x, 1), device_id_type=MESH)
        pl.when(c == 0)(base_copy.start)
        direct_copy = pltpu.make_async_remote_copy(
            src_ref=prefix.at[ahead[nx - 2], own - 1], dst_ref=direct.at[1], send_sem=p_send, recv_sem=d_recv.at[1],
            device_id=device(ahead[nx - 2], 1), device_id_type=MESH)

    q_copy.wait()

    def head_of(side, s, p):
        owner = x if s == nx - 1 else behind[s]
        return (o if side else c) * half + owner * own + p

    def local(batch):
        for one in batch:
            head = head_of(*one)
            qq = silu(qb[:, cols(head)])
            scores = lax.dot_general(qq, kb[:, cols(head)], (((1,), (1,)), ((), ())), preferred_element_type=F32)
            wq[head, :, :rows] = scores.astype(BF16) * maskb[...]
            wq[head, :, rows:] = qq * joinb[...]

    @pl.when(z == 0)
    def _():
        zin[...] = jnp.zeros_like(zin)

    @pl.when((z == 0) & (x == 0))
    def _():
        pin[...] = jnp.zeros_like(pin)
        direct[1] = jnp.zeros_like(direct[1])

    def z_copy(p):
        return pltpu.make_async_remote_copy(
            src_ref=zout.at[p], dst_ref=zin.at[p], send_sem=z_send, recv_sem=z_recv.at[p],
            device_id=device(x, c, z + 1), device_id_type=MESH)

    def receive(p):
        @pl.when(z > 0)
        def _():
            z_copy(p).wait_recv()

    def fold(p):
        for s in range(nx - 1):
            coming = (z < nz - 1) | (behind[s] < nx - 1)
            if s == 0 and p == 0:
                for cp in e_copies:
                    pl.when(coming)(cp.wait_recv)
                tin[0, 0] = (early[1].astype(F32) + early[0].astype(F32) * other).astype(BF16)
                continue
            pl.when(coming)(t_copies[s, p].wait_recv)
        add = None
        for xx in range(nx):
            got = tin[lax.rem(x + 2 * nx - 1 - xx, nx), p].astype(F32)
            add = got if xx == 0 else got + add * cont[xx]
            partial[p, xx] = add
        if chained:
            receive(p)
            whole = 1.0
            for xx in range(nx):
                whole = whole * cont[xx]
            add = add + zin[p].astype(F32) * whole
        zout[p] = add.astype(BF16)

        @pl.when(z < nz - 1)
        def _():
            z_copy(p).start()

    p_copies = {}
    f_copies = {}

    def forward(s, p, state):
        into = tt[0, nx - 1 if s == nx - 1 else nx - 2 - s, p].astype(F32) + state.astype(F32) * low
        st[0, s, p] = state
        st[1, s, p] = into.astype(BF16)
        cp = pltpu.make_async_remote_copy(
            src_ref=st.at[o, s, p], dst_ref=fin.at[s * own + p], send_sem=s_send, recv_sem=f_recv.at[s, p],
            device_id=device(x, o), device_id_type=MESH)
        if (s, p) == last:
            pl.when(c > 0)(cp.start)
        else:
            cp.start()
        f_copies[s, p] = cp

    def spread(p):
        if not chained:
            receive(p)
        carried = zin[p].astype(F32)
        passed = 1.0
        prefix[0, p] = zin[p]
        for xx in range(nx - 1):
            passed = passed * cont[xx]
            prefix[xx + 1, p] = (partial[p, xx] + carried * passed).astype(BF16)
        for s in range(nx - 1):
            if (s, p) == last:
                pl.when((c == 0) & ((z > 0) | (ahead[s] > 0)))(direct_copy.start)
            cp = pltpu.make_async_remote_copy(
                src_ref=prefix.at[ahead[s], p], dst_ref=pin.at[s * own + p],
                send_sem=p_send, recv_sem=p_recv.at[s, p],
                device_id=device(ahead[s], c), device_id_type=MESH)
            pl.when((z > 0) | (ahead[s] > 0))(cp.start)
            p_copies[s, p] = cp
        forward(nx - 1, p, prefix[x, p])

    def finish(batch, total):
        for side, s, p in batch:
            if side and (s, p) == last:
                pl.when(c == 0)(f_copies[s, p].wait_recv)

                @pl.when(c > 0)
                def _():
                    base_copy.wait_recv()
                    pl.when((z > 0) | (x > 0))(direct_copy.wait_recv)
                    fin[s * own + p] = (direct[0].astype(F32) + direct[1].astype(F32) * low).astype(BF16)
            elif side:
                f_copies[s, p].wait_recv()
        for side, s, p in batch:
            head = head_of(side, s, p)
            state = fin[s * own + p] if side else st[c, s, p]
            both = jnp.concatenate([vb[:, cols(head)], state], axis=0)
            att = jnp.dot(wq[head], both, preferred_element_type=F32).astype(BF16)
            out_ref[:, cols(head)] = att
            att = att.astype(F32)
            total = total + att * att
        return total

    lag = 0 if chained else min(3, own)
    rest = [(s, p) for s in range(nx - 1) for p in range(own)]
    every = [(side, s, p) for s, p in [(nx - 1, p) for p in range(own)] + rest for side in (0, 1)]
    ready = {}
    for n in range(own):
        ready[0, nx - 1, n] = n + lag
        ready[1, nx - 1, n] = n + lag + LATE
    for n, (s, p) in enumerate(rest):
        ready[0, s, p] = n + own
        ready[1, s, p] = n + own + LATE
    slots = own + len(rest)
    waiting = sorted(ready, key=lambda one: (ready[one], one))
    todo = list(every)
    total = jnp.zeros((rows, DH), F32)
    for slot in range(slots):
        if slot < own:
            fold(slot)
        count = -(-len(todo) // max(own - slot, 1))
        local(todo[:count])
        todo = todo[count:]
        if lag <= slot < own + lag:
            spread(slot - lag)
        if slot >= own:
            s, p = rest[slot - own]
            pl.when((z > 0) | (x > 0))(p_copies[s, p].wait_recv)
            forward(s, p, pin[s * own + p])
        now = [one for one in waiting if ready[one] <= slot and one not in todo]
        if len(now) >= (BATCH if slot < own else 2):
            total = finish(now[:BATCH], total)
            waiting = [one for one in waiting if one not in now[:BATCH]]
    sums[...] = total

    @pl.when(c == 0)
    def _():
        sums[...] = finish(waiting, sums[...])

    @pl.when(c > 0)
    def _():
        ends_with = [(1, *one) for one in rest[-1:] + rest[-2:-1]]
        others = [one for one in waiting if one not in ends_with]
        sums[...] = finish(others, sums[...])
        for one in ends_with:
            sums[...] = finish([one], sums[...])

    total = sums[...]
    scale = lax.rsqrt(jnp.sum(total, axis=1, keepdims=True) / width + 1e-05)
    scale_ref[...] = jnp.broadcast_to(scale, (rows, DH))

    def sent(src, dst, sem, recv):
        pltpu.make_async_remote_copy(
            src_ref=src, dst_ref=dst, send_sem=sem, recv_sem=recv,
            device_id=device(x, o), device_id_type=MESH).wait_send()

    def sent_if(cond, count, sem):
        if count > 0:
            @pl.when(cond)
            def _():
                part = pl.ds(0, count)
                sent(fin.at[part], fin.at[part], sem, s_recv.at[0])

    sent(tt, tt, s_send, s_recv.at[0])
    if nx > 1:
        sent_if(tails_used, (nx - 1) * own + 1, t_send)
        whole = (z > 0) | (x == 0)
        straight = (c == 0) & ((z > 0) | (ahead[nx - 2] > 0))
        for cond, count in ((whole, (nx - 1) * own), (~whole, (nx - 2) * own)):
            sent_if(cond & straight, count + 1, p_send)
            sent_if(cond & ~straight, count, p_send)

    @pl.when(z < nz - 1)
    def _():
        sent(zout, zin, z_send, z_recv.at[0])


def scale_kernel(parts, att_ref, scale_ref, gain_ref, out_hbm, buf, sem):
    rows, width = att_ref.shape
    part = rows // parts
    for j in range(parts):
        at = pl.ds(j * part, part)
        scale = scale_ref[at, :]
        for i in range(width // DH):
            col = pl.ds(i * DH, DH)
            v = att_ref[at, col].astype(F32)
            buf[at, col] = (v * scale * gain_ref[0:1, col]).astype(BF16)
        pltpu.make_async_copy(buf.at[at], out_hbm.at[at], sem).start()
    pltpu.make_async_copy(buf, out_hbm, sem).wait()


def per_device(nz, nh, queries, keys_in, values, doc_lengths, rms_gain):
    rows, width = queries.shape
    nx = nh // 2
    heads = width // DH
    own = heads // 2 // nx
    group = 2 if own % 2 == 0 else 1
    groups = own // group
    far = max(nx - 1, 1)
    docs = doc_lengths.shape
    vmem = pltpu.VMEM
    full = vmem((rows, width), BF16)
    dma = pltpu.SemaphoreType.DMA
    hbm_spec = pl.BlockSpec(memory_space=pltpu.HBM)
    vmem_spec = pl.BlockSpec(memory_space=pltpu.VMEM)
    attended, scale = pl.pallas_call(
        functools.partial(kernel, nz, nh, group),
        out_shape=(jax.ShapeDtypeStruct((rows, width), BF16), jax.ShapeDtypeStruct((rows, DH), F32)),
        in_specs=[hbm_spec] * 4,
        out_specs=(vmem_spec, vmem_spec),
        scratch_shapes=[
            pltpu.SMEM(docs, jnp.int32), dma(()),
            full, full, full,
            vmem((heads, rows, rows + DH), BF16),
            vmem((rows, rows), BF16),
            vmem((rows, DH), BF16),
            vmem((rows, DH), BF16),
            vmem((nx, own, DH, DH), BF16),
            vmem((2, nx, own, DH, DH), BF16),
            vmem((far * own, DH, DH), BF16),
            vmem((nx, own, DH, DH), BF16),
            vmem((own, nx, DH, DH), F32),
            vmem((own, DH, DH), BF16),
            vmem((own, DH, DH), BF16),
            vmem((nx, own, DH, DH), BF16),
            vmem((far * own, DH, DH), BF16),
            vmem((2, nx, own, DH, DH), BF16),
            vmem((nx * own, DH, DH), BF16),
            vmem((2, DH, DH), BF16),
            vmem((2, DH, DH), BF16),
            vmem((rows, DH), F32),
            dma((nx + 2,)),
            dma(()), dma((groups + (nx - 1) * (groups // (2 if groups % 2 == 0 else 1)),)),
            dma(()), dma((far, own)),
            dma(()), dma((own,)),
            dma(()), dma((far, own)),
            dma((nx, own)),
            dma(()),
            dma((2,)),
        ],
        compiler_params=pltpu.CompilerParams(collective_id=0, has_side_effects=True, vmem_limit_bytes=LIMIT1),
        name="scan_attention",
    )(pltpu.with_memory_space_constraint(doc_lengths, pltpu.HBM), queries, keys_in, values)
    parts = 8
    return pl.pallas_call(
        functools.partial(scale_kernel, parts),
        out_shape=jax.ShapeDtypeStruct((rows, width), BF16),
        in_specs=[pl.BlockSpec(memory_space=pltpu.VMEM)] * 3,
        out_specs=pl.BlockSpec(memory_space=pl.ANY),
        scratch_shapes=[pltpu.VMEM((rows, width), BF16), dma(())],
        compiler_params=pltpu.CompilerParams(vmem_limit_bytes=LIMIT2),
        name="scale_rows",
    )(attended, scale, rms_gain.reshape(1, width))


def solution(mesh):
    split = P(("groups", "ctx", "head"), None)
    return jax.shard_map(
        functools.partial(per_device, mesh.shape["ctx"], mesh.shape["head"]),
        mesh=mesh,
        in_specs=(split, split, split, P("groups"), P()),
        out_specs=split,
        check_vma=False,
    )
```

```python
import functools

import jax
import jax.numpy as jnp
from jax import lax
from jax.experimental import pallas as pl
from jax.experimental.pallas import tpu as pltpu
from jax.sharding import PartitionSpec as P

DH = 128
MESH = pl.DeviceIdType.MESH
LIMIT1 = 52 << 20
LIMIT2 = 8 << 20
F32 = jnp.float32
BF16 = jnp.bfloat16
BATCH = 4
LATE = 3


def silu(v):
    v = v.astype(F32)
    half = 0.5 * v
    return (half + half * jnp.tanh(half)).astype(BF16)


def kernel(nz, nh, group, docs_hbm, q_hbm, k_hbm, v_hbm, out_ref, scale_ref,
           ends_ref, doc_sem, qb, kb, vb, wq, maskb, joinb, keepb, tsend, tt, xout, tin, partial, zin, zout, prefix, pin, st, fin, early, direct, sums,
           load_sem, s_send, s_recv, t_send, t_recv, z_send, z_recv, p_send, p_recv, f_recv, e_recv, d_recv):
    nx = nh // 2
    rows, width = q_hbm.shape
    heads = width // DH
    half = heads // 2
    own = half // nx
    docs = ends_ref.shape[0]
    chunk = 2 * rows
    shard = nx * chunk
    longest = nz * shard // nh
    chained = longest > shard
    z = lax.axis_index("ctx")
    h = lax.axis_index("head")
    x = h // 2
    c = h % 2
    o = 1 - c

    def device(xx, cc, zz=None):
        return {"ctx": z if zz is None else zz, "head": 2 * xx + cc}

    ahead = [lax.rem(x + 1 + s, nx) for s in range(nx)]
    behind = [lax.rem(x + 2 * nx - 1 - s, nx) for s in range(nx)]

    def cols(head, count=1):
        return pl.ds(pl.multiple_of(head * DH, DH), count * DH)

    def first_head(side, s, g):
        return (o if side else c) * half + ahead[s] * own + g * group

    groups = own // group

    tails_used = (z < nz - 1) | (x < nx - 1)

    def load(side, s, g, count, sem):
        at = cols(first_head(side, s, g), count)
        for src, dst in ((k_hbm, kb), (v_hbm, vb)):
            pltpu.make_async_copy(src.at[:, at], dst.at[:, at], load_sem.at[sem]).start()

    def loaded(sem, count):
        at = pl.ds(0, 4 * count * DH)
        pltpu.make_async_copy(k_hbm.at[:, at], kb.at[:, at], load_sem.at[sem]).wait()

    for side in (1, 0):
        load(side, 0, 0, group, 0)
    docs_copy = pltpu.make_async_copy(docs_hbm, ends_ref, doc_sem)
    docs_copy.start()

    barrier = pltpu.get_barrier_semaphore()
    pl.semaphore_signal(barrier, inc=1, device_id=device(x, o), device_id_type=MESH)
    for s in range(nx - 1):
        pl.semaphore_signal(barrier, inc=1, device_id=device(ahead[s], c), device_id_type=MESH)

    across = [ahead[0], behind[0]][:min(nx - 1, 2)]
    for xx in across:
        pl.semaphore_signal(barrier, inc=1, device_id=device(xx, o), device_id_type=MESH)

    @pl.when(z > 0)
    def _():
        pl.semaphore_signal(barrier, inc=1, device_id=device(x, c, z - 1), device_id_type=MESH)

    @pl.when(z < nz - 1)
    def _():
        pl.semaphore_signal(barrier, inc=1, device_id=device(x, c, z + 1), device_id_type=MESH)

    for s in range(nx):
        skip = 0 if s else 1
        if groups > skip:
            for side in (1, 0):
                load(side, s, skip, own - skip * group, s + 1)
    q_copy = pltpu.make_async_copy(q_hbm, qb, load_sem.at[nx + 1])
    q_copy.start()

    def activate(i):
        for side in (1, 0):
            at = cols(first_head(side, 0, 0) + i)
            kb[:, at] = silu(kb[:, at])

    loaded(0, group)
    activate(0)
    docs_copy.wait()
    ends = [ends_ref[0]]
    for d in range(1, docs):
        ends.append(ends[-1] + ends_ref[d])

    def seg_of(pos):
        total = jnp.where(pos < 0, -1, 0)
        for end in ends:
            total = total + jnp.where(pos >= end, 1, 0)
        return total

    def spans(start, count):
        return jnp.where(seg_of(start - 1) == seg_of(start + count - 1), 1.0, 0.0).astype(F32)

    shard_start = z * shard
    chip = shard_start + x * chunk
    first = chip + c * rows
    row_i = lax.broadcasted_iota(jnp.int32, (rows, DH), 0)
    seg_r = seg_of(row_i + first)
    keepb[...] = jnp.where(seg_r == seg_of(first + rows - 1), 1.0, 0.0).astype(BF16)

    def tails(s, g, begin=0, end=None):
        if s == 0 and g == 1:
            loaded(1, own - group)
        elif s and g == 0:
            loaded(s + 1, own)
        for i in range(begin, group if end is None else end):
            for side in (1, 0):
                at = cols(first_head(side, s, g) + i)
                kk = kb[:, at] if s == 0 and g == 0 and i == 0 else silu(kb[:, at])
                kb[:, at] = kk
                t = lax.dot_general(kk * keepb[...], vb[:, at], (((0,), (0,)), ((), ())), preferred_element_type=F32).astype(BF16)
                if side:
                    tsend[s, g * group + i] = t
                else:
                    tt[c, s, g * group + i] = t

    s_copies = {}
    wide = 4 if groups % 4 == 0 else 1

    def pass_tails(s, g):
        count = wide if s else 1
        at = pl.ds((g + 1 - count) * group, count * group)
        cp = pltpu.make_async_remote_copy(
            src_ref=tsend.at[s, at], dst_ref=tt.at[c, s, at], send_sem=s_send, recv_sem=s_recv.at[g if s == 0 else groups + (s - 1) * (groups // wide) + g // wide],
            device_id=device(x, o), device_id_type=MESH)
        cp.start()
        s_copies[s, g] = cp

    t_copies = {}

    def join_tails(s, g):
        if s == 0 or g % wide == 0:
            s_copies[s, g if s == 0 else g + wide - 1].wait_recv()
        for i in range(group):
            p = g * group + i
            if s == 0 and p == 0 and nx > 1:
                continue
            t = (tt[1, s, p].astype(F32) + tt[0, s, p].astype(F32) * high).astype(BF16)
            if s == nx - 1:
                tin[s, p] = t
                continue
            xout[s * own + p] = t
            cp = pltpu.make_async_remote_copy(
                src_ref=xout.at[s * own + p], dst_ref=tin.at[s, p], send_sem=t_send, recv_sem=t_recv.at[s, p],
                device_id=device(ahead[s], c), device_id_type=MESH)
            pl.when(tails_used)(cp.start)
            t_copies[s, p] = cp

    tails(0, 0, 0, 1)
    pl.semaphore_wait(barrier, nx + len(across) + jnp.where(z > 0, 1, 0) + jnp.where(z < nz - 1, 1, 0))
    e_copies = []
    if nx > 1:
        for n, (src, cc) in enumerate(((tt.at[c, 0, 0], c), (tsend.at[0, 0], o))):
            cp = pltpu.make_async_remote_copy(
                src_ref=src, dst_ref=early.at[c], send_sem=t_send, recv_sem=t_recv.at[0, 0] if n == 0 else e_recv,
                device_id=device(ahead[0], cc), device_id_type=MESH)
            pl.when(tails_used)(cp.start)
            e_copies.append(cp)
    tails(0, 0, 1)
    pass_tails(0, 0)
    joinb[...] = jnp.where(seg_r == seg_of(first - 1), 1.0, 0.0).astype(BF16)
    col_i = lax.broadcasted_iota(jnp.int32, (8, rows), 1)
    seg_c = seg_of(col_i + first)[0:1]
    for g in range(rows // DH):
        sc = jnp.broadcast_to(seg_c[:, g * DH:(g + 1) * DH], (rows, DH))
        ci = lax.broadcasted_iota(jnp.int32, (rows, DH), 1) + g * DH
        maskb[:, g * DH:(g + 1) * DH] = jnp.where((seg_r == sc) & (row_i >= ci), 1.0, 0.0).astype(BF16)
    low = spans(chip, rows)
    high = spans(chip + rows, rows)
    other = spans(shard_start + behind[0] * chunk + rows, rows)
    cont = [spans(shard_start + xx * chunk, chunk) for xx in range(nx)]

    order = [(s, g) for s in range(nx) for g in range(groups)]
    delay = min(3, len(order) - 1)
    for n, (s, g) in enumerate(order):
        if n:
            tails(s, g)
            if s == 0 or g % wide == wide - 1:
                pass_tails(s, g)
        if n >= delay:
            join_tails(*order[n - delay])
    for s, g in order[len(order) - delay:]:
        join_tails(s, g)

    last = (nx - 2, own - 1) if nx > 1 else None
    if nx > 1:
        base_copy = pltpu.make_async_remote_copy(
            src_ref=tt.at[0, 0, own - 1], dst_ref=direct.at[0], send_sem=s_send, recv_sem=d_recv.at[0],
            device_id=device(x, 1), device_id_type=MESH)
        pl.when(c == 0)(base_copy.start)
        direct_copy = pltpu.make_async_remote_copy(
            src_ref=prefix.at[ahead[nx - 2], own - 1], dst_ref=direct.at[1], send_sem=p_send, recv_sem=d_recv.at[1],
            device_id=device(ahead[nx - 2], 1), device_id_type=MESH)

    q_copy.wait()

    def head_of(side, s, p):
        owner = x if s == nx - 1 else behind[s]
        return (o if side else c) * half + owner * own + p

    def local(batch):
        for one in batch:
            head = head_of(*one)
            qq = silu(qb[:, cols(head)])
            scores = lax.dot_general(qq, kb[:, cols(head)], (((1,), (1,)), ((), ())), preferred_element_type=F32)
            wq[head, :, :rows] = scores.astype(BF16) * maskb[...]
            wq[head, :, rows:] = qq * joinb[...]

    @pl.when(z == 0)
    def _():
        zin[...] = jnp.zeros_like(zin)

    @pl.when((z == 0) & (x == 0))
    def _():
        pin[...] = jnp.zeros_like(pin)
        direct[1] = jnp.zeros_like(direct[1])

    def z_copy(p):
        return pltpu.make_async_remote_copy(
            src_ref=zout.at[p], dst_ref=zin.at[p], send_sem=z_send, recv_sem=z_recv.at[p],
            device_id=device(x, c, z + 1), device_id_type=MESH)

    def receive(p):
        @pl.when(z > 0)
        def _():
            z_copy(p).wait_recv()

    def fold(p):
        for s in range(nx - 1):
            coming = (z < nz - 1) | (behind[s] < nx - 1)
            if s == 0 and p == 0:
                for cp in e_copies:
                    pl.when(coming)(cp.wait_recv)
                tin[0, 0] = (early[1].astype(F32) + early[0].astype(F32) * other).astype(BF16)
                continue
            pl.when(coming)(t_copies[s, p].wait_recv)
        add = None
        for xx in range(nx):
            got = tin[lax.rem(x + 2 * nx - 1 - xx, nx), p].astype(F32)
            add = got if xx == 0 else got + add * cont[xx]
            partial[p, xx] = add
        if chained:
            receive(p)
            whole = 1.0
            for xx in range(nx):
                whole = whole * cont[xx]
            add = add + zin[p].astype(F32) * whole
        zout[p] = add.astype(BF16)

        @pl.when(z < nz - 1)
        def _():
            z_copy(p).start()

    p_copies = {}
    f_copies = {}

    def forward(s, p, state):
        into = tt[0, nx - 1 if s == nx - 1 else nx - 2 - s, p].astype(F32) + state.astype(F32) * low
        st[0, s, p] = state
        st[1, s, p] = into.astype(BF16)
        cp = pltpu.make_async_remote_copy(
            src_ref=st.at[o, s, p], dst_ref=fin.at[s * own + p], send_sem=s_send, recv_sem=f_recv.at[s, p],
            device_id=device(x, o), device_id_type=MESH)
        if (s, p) == last:
            pl.when(c > 0)(cp.start)
        else:
            cp.start()
        f_copies[s, p] = cp

    def spread(p):
        if not chained:
            receive(p)
        carried = zin[p].astype(F32)
        passed = 1.0
        prefix[0, p] = zin[p]
        for xx in range(nx - 1):
            passed = passed * cont[xx]
            prefix[xx + 1, p] = (partial[p, xx] + carried * passed).astype(BF16)
        for s in range(nx - 1):
            if (s, p) == last:
                pl.when((c == 0) & ((z > 0) | (ahead[s] > 0)))(direct_copy.start)
            cp = pltpu.make_async_remote_copy(
                src_ref=prefix.at[ahead[s], p], dst_ref=pin.at[s * own + p],
                send_sem=p_send, recv_sem=p_recv.at[s, p],
                device_id=device(ahead[s], c), device_id_type=MESH)
            pl.when((z > 0) | (ahead[s] > 0))(cp.start)
            p_copies[s, p] = cp
        forward(nx - 1, p, prefix[x, p])

    def finish(batch, total):
        for side, s, p in batch:
            if side and (s, p) == last:
                pl.when(c == 0)(f_copies[s, p].wait_recv)

                @pl.when(c > 0)
                def _():
                    base_copy.wait_recv()
                    pl.when((z > 0) | (x > 0))(direct_copy.wait_recv)
                    fin[s * own + p] = (direct[0].astype(F32) + direct[1].astype(F32) * low).astype(BF16)
            elif side:
                f_copies[s, p].wait_recv()
        for side, s, p in batch:
            head = head_of(side, s, p)
            state = fin[s * own + p] if side else st[c, s, p]
            both = jnp.concatenate([vb[:, cols(head)], state], axis=0)
            att = jnp.dot(wq[head], both, preferred_element_type=F32).astype(BF16)
            out_ref[:, cols(head)] = att
            att = att.astype(F32)
            total = total + att * att
        return total

    lag = 0 if chained else min(3, own)
    rest = [(s, p) for s in range(nx - 1) for p in range(own)]
    every = [(side, s, p) for s, p in [(nx - 1, p) for p in range(own)] + rest for side in (0, 1)]
    ready = {}
    for n in range(own):
        ready[0, nx - 1, n] = n + lag
        ready[1, nx - 1, n] = n + lag + LATE
    for n, (s, p) in enumerate(rest):
        ready[0, s, p] = n + own
        ready[1, s, p] = n + own + LATE
    slots = own + len(rest)
    waiting = sorted(ready, key=lambda one: (ready[one], one))
    todo = list(every)
    total = jnp.zeros((rows, DH), F32)
    for slot in range(slots):
        if slot < own:
            fold(slot)
        count = -(-len(todo) // max(own - slot, 1))
        local(todo[:count])
        todo = todo[count:]
        if lag <= slot < own + lag:
            spread(slot - lag)
        if slot >= own:
            s, p = rest[slot - own]
            pl.when((z > 0) | (x > 0))(p_copies[s, p].wait_recv)
            forward(s, p, pin[s * own + p])
        now = [one for one in waiting if ready[one] <= slot and one not in todo]
        if len(now) >= (BATCH if slot < own else 2):
            total = finish(now[:BATCH], total)
            waiting = [one for one in waiting if one not in now[:BATCH]]
    sums[...] = total

    @pl.when(c == 0)
    def _():
        sums[...] = finish(waiting, sums[...])

    @pl.when(c > 0)
    def _():
        ends_with = [(1, *one) for one in rest[-1:] + rest[-2:-1]]
        others = [one for one in waiting if one not in ends_with]
        sums[...] = finish(others, sums[...])
        for one in ends_with:
            sums[...] = finish([one], sums[...])

    total = sums[...]
    scale = lax.rsqrt(jnp.sum(total, axis=1, keepdims=True) / width + 1e-05)
    scale_ref[...] = jnp.broadcast_to(scale, (rows, DH))

    def sent(src, dst, sem, recv):
        pltpu.make_async_remote_copy(
            src_ref=src, dst_ref=dst, send_sem=sem, recv_sem=recv,
            device_id=device(x, o), device_id_type=MESH).wait_send()

    def sent_if(cond, count, sem):
        if count > 0:
            @pl.when(cond)
            def _():
                part = pl.ds(0, count)
                sent(fin.at[part], fin.at[part], sem, s_recv.at[0])

    sent(tt, tt, s_send, s_recv.at[0])
    if nx > 1:
        sent_if(tails_used, (nx - 1) * own + 1, t_send)
        whole = (z > 0) | (x == 0)
        straight = (c == 0) & ((z > 0) | (ahead[nx - 2] > 0))
        for cond, count in ((whole, (nx - 1) * own), (~whole, (nx - 2) * own)):
            sent_if(cond & straight, count + 1, p_send)
            sent_if(cond & ~straight, count, p_send)

    @pl.when(z < nz - 1)
    def _():
        sent(zout, zin, z_send, z_recv.at[0])


def scale_kernel(parts, att_ref, scale_ref, gain_ref, out_hbm, buf, sem):
    rows, width = att_ref.shape
    part = rows // parts
    for j in range(parts):
        at = pl.ds(j * part, part)
        scale = scale_ref[at, :]
        for i in range(width // DH):
            col = pl.ds(i * DH, DH)
            v = att_ref[at, col].astype(F32)
            buf[at, col] = (v * scale * gain_ref[0:1, col]).astype(BF16)
        pltpu.make_async_copy(buf.at[at], out_hbm.at[at], sem).start()
    pltpu.make_async_copy(buf, out_hbm, sem).wait()


def per_device(nz, nh, queries, keys_in, values, doc_lengths, rms_gain):
    rows, width = queries.shape
    nx = nh // 2
    heads = width // DH
    own = heads // 2 // nx
    group = 2 if own % 2 == 0 else 1
    groups = own // group
    far = max(nx - 1, 1)
    docs = doc_lengths.shape
    vmem = pltpu.VMEM
    full = vmem((rows, width), BF16)
    dma = pltpu.SemaphoreType.DMA
    hbm_spec = pl.BlockSpec(memory_space=pltpu.HBM)
    vmem_spec = pl.BlockSpec(memory_space=pltpu.VMEM)
    attended, scale = pl.pallas_call(
        functools.partial(kernel, nz, nh, group),
        out_shape=(jax.ShapeDtypeStruct((rows, width), BF16), jax.ShapeDtypeStruct((rows, DH), F32)),
        in_specs=[hbm_spec] * 4,
        out_specs=(vmem_spec, vmem_spec),
        scratch_shapes=[
            pltpu.SMEM(docs, jnp.int32), dma(()),
            full, full, full,
            vmem((heads, rows, rows + DH), BF16),
            vmem((rows, rows), BF16),
            vmem((rows, DH), BF16),
            vmem((rows, DH), BF16),
            vmem((nx, own, DH, DH), BF16),
            vmem((2, nx, own, DH, DH), BF16),
            vmem((far * own, DH, DH), BF16),
            vmem((nx, own, DH, DH), BF16),
            vmem((own, nx, DH, DH), F32),
            vmem((own, DH, DH), BF16),
            vmem((own, DH, DH), BF16),
            vmem((nx, own, DH, DH), BF16),
            vmem((far * own, DH, DH), BF16),
            vmem((2, nx, own, DH, DH), BF16),
            vmem((nx * own, DH, DH), BF16),
            vmem((2, DH, DH), BF16),
            vmem((2, DH, DH), BF16),
            vmem((rows, DH), F32),
            dma((nx + 2,)),
            dma(()), dma((groups + (nx - 1) * (groups // (4 if groups % 4 == 0 else 1)),)),
            dma(()), dma((far, own)),
            dma(()), dma((own,)),
            dma(()), dma((far, own)),
            dma((nx, own)),
            dma(()),
            dma((2,)),
        ],
        compiler_params=pltpu.CompilerParams(collective_id=0, has_side_effects=True, vmem_limit_bytes=LIMIT1),
        name="scan_attention",
    )(pltpu.with_memory_space_constraint(doc_lengths, pltpu.HBM), queries, keys_in, values)
    parts = 8
    return pl.pallas_call(
        functools.partial(scale_kernel, parts),
        out_shape=jax.ShapeDtypeStruct((rows, width), BF16),
        in_specs=[pl.BlockSpec(memory_space=pltpu.VMEM)] * 3,
        out_specs=pl.BlockSpec(memory_space=pl.ANY),
        scratch_shapes=[pltpu.VMEM((rows, width), BF16), dma(())],
        compiler_params=pltpu.CompilerParams(vmem_limit_bytes=LIMIT2),
        name="scale_rows",
    )(attended, scale, rms_gain.reshape(1, width))


def solution(mesh):
    split = P(("groups", "ctx", "head"), None)
    return jax.shard_map(
        functools.partial(per_device, mesh.shape["ctx"], mesh.shape["head"]),
        mesh=mesh,
        in_specs=(split, split, split, P("groups"), P()),
        out_specs=split,
        check_vma=False,
    )
```
